256 devices in a mesh: seq: 64 (over z, x, core), head: 4 (over y).
Axes of the slice: x: 4, y: 4, z: 8, core: 2. Of those that a mesh axis runs over, the one named last changes fastest.
Arguments:
- queries: bfloat16 [32768, 4096], P('seq', 'head'), may hold values from -6 to 6
- keys: bfloat16 [32768, 4096], P('seq', 'head'), may hold values from -6 to 6
- values: bfloat16 [32768, 4096], P('seq', 'head'), may hold values from -6 to 6
- med_weight: float32 [2, 32, 4], P(None, 'head'), may hold values from -3 to 3
- coarse_weight: float32 [2, 32, 64], P(None, 'head'), may hold values from -0.75 to 0.75
- out_weight: bfloat16 [4096, 4096], P('head'), may hold values from -0.09375 to 0.09375
Outputs:
- mixed: bfloat16 [32768, 4096], P('seq', 'head')
The draws below stay inside these ranges and needn't reach their ends.
All inputs are finite; a program needn't handle non-finite values.
Results may differ from the reference program's by a relative error of at most 0.013.
Values may be sent and summed in bfloat16 or wider, within the bound.
No kernel may reach another device: no remote copies, remote signals or barrier semaphores. Data moves between devices by JAX's collectives and lax.ppermute only.
A program may use at most 128 MiB of HBM per device.

```python
import math
import jax
import jax.numpy as jnp
from jax import lax

D = 4096
HEADS = 32
HEAD_DIM = 128
TOK_DEV = 512
WIN = 512
MED = 4
COARSE = 64
TOKENS = 32768
N_SEQ = 64
N_HEAD = 4


def draw_queries(key, part):
    noise_key = jax.random.fold_in(key, 11)
    draws_bulk = jnp.clip(jax.random.normal(noise_key, (TOKENS, HEADS * HEAD_DIM), jnp.float32), -6.0, 6.0)
    return draws_bulk.astype(jnp.bfloat16)


def draw_keys(key, part):
    noise_key = jax.random.fold_in(key, 23)
    draws_bulk = jnp.clip(jax.random.normal(noise_key, (TOKENS, HEADS * HEAD_DIM), jnp.float32), -6.0, 6.0)
    return draws_bulk.astype(jnp.bfloat16)


def block_levels(stream_key, dims, cuts, smallest, top_value):
    def one(dim, shards_of):
        steps = jax.random.uniform(jax.random.fold_in(jax.random.fold_in(stream_key, 6), dim), (shards_of,), jnp.float32, smallest / len(cuts), top_value / len(cuts))
        return jnp.repeat(jnp.exp(steps), dims[dim] // shards_of).reshape((-1,) + (1,) * (len(dims) - dim - 1))

    gain = one(*cuts[0])
    for cut in cuts[1:]:
        gain = gain * one(*cut)
    return gain


def normal_values(stream_key, extent, spread, reach, pieces=(), kind=jnp.bfloat16):
    values = spread * jax.random.normal(stream_key, extent, jnp.float32)
    if pieces:
        values = values * block_levels(stream_key, extent, pieces, -0.22, 0.18)
    return jnp.clip(values, -reach, reach).astype(kind)


def setup_inputs(seed: int = 0) -> dict:
    arg_keys = jax.random.split(jax.random.key(seed), 7)
    queries = draw_queries(jax.random.fold_in(arg_keys[6], 71), 0)
    keys = draw_keys(jax.random.fold_in(arg_keys[6], 71), 0)
    values = normal_values(arg_keys[2], (TOKENS, HEADS * HEAD_DIM), 1.0, 6.0, ((0, 64), (1, 4)))
    med_weight = normal_values(arg_keys[3], (2, HEADS, MED), MED ** -0.5, 3.0, ((1, 4),), jnp.float32)
    coarse_weight = normal_values(arg_keys[4], (2, HEADS, COARSE), COARSE ** -0.5, 0.75, ((1, 4),), jnp.float32)
    out_weight = normal_values(arg_keys[5], (HEADS * HEAD_DIM, D), (HEADS * HEAD_DIM) ** -0.5, 0.09375, ((0, 4),))
    return dict(queries=queries, keys=keys, values=values, med_weight=med_weight, coarse_weight=coarse_weight, out_weight=out_weight)


def summarize(tensor, weight, ratio):
    groups = tensor.shape[0] // ratio
    grouped = tensor.reshape(groups, ratio, tensor.shape[1], tensor.shape[2]).astype(jnp.float32)
    return jnp.einsum('jrhd,hr->jhd', grouped, weight.astype(jnp.float32)).astype(jnp.bfloat16)

def reference(queries, keys, values, med_weight, coarse_weight, out_weight):
    head_width = HEAD_DIM
    query3 = queries.reshape(TOKENS, HEADS, head_width)
    key3 = keys.reshape(TOKENS, HEADS, head_width)
    value3 = values.reshape(TOKENS, HEADS, head_width)
    med_keys = summarize(key3, med_weight[0], MED)
    med_values = summarize(value3, med_weight[1], MED)
    coarse_keys = summarize(key3, coarse_weight[0], COARSE)
    coarse_values = summarize(value3, coarse_weight[1], COARSE)
    per_med = TOK_DEV // MED
    per_coarse = TOK_DEV // COARSE
    group_width = HEADS * head_width // N_HEAD
    score_scale = 1.0 / math.sqrt(head_width)
    coarse_owner = jnp.arange(TOKENS // COARSE, dtype=jnp.int32) // per_coarse

    def one_block(position):
        first = position * TOK_DEV
        query_blk = lax.dynamic_slice_in_dim(query3, first, TOK_DEV, 0)
        edge_first = jnp.maximum(first - WIN, 0).astype(jnp.int32)
        key_list = [lax.dynamic_slice_in_dim(key3, first, TOK_DEV, 0), lax.dynamic_slice_in_dim(key3, edge_first, WIN, 0)]
        value_list = [lax.dynamic_slice_in_dim(value3, first, TOK_DEV, 0), lax.dynamic_slice_in_dim(value3, edge_first, WIN, 0)]
        place_list = [jnp.arange(TOK_DEV, dtype=jnp.int32), jnp.full((WIN,), -1, jnp.int32)]
        usable_list = [jnp.ones((TOK_DEV,), bool), jnp.broadcast_to(position >= 1, (WIN,))]
        for distance in (2, 3, 4):
            med_first = (jnp.maximum(position - distance, 0) * per_med).astype(jnp.int32)
            key_list.append(lax.dynamic_slice_in_dim(med_keys, med_first, per_med, 0))
            value_list.append(lax.dynamic_slice_in_dim(med_values, med_first, per_med, 0))
            place_list.append(jnp.full((per_med,), -1, jnp.int32))
            usable_list.append(jnp.broadcast_to(position >= distance, (per_med,)))
        key_list.append(coarse_keys)
        value_list.append(coarse_values)
        place_list.append(jnp.full((TOKENS // COARSE,), -1, jnp.int32))
        usable_list.append(coarse_owner <= position - 1)
        key_all = jnp.concatenate(key_list, 0)
        value_all = jnp.concatenate(value_list, 0)
        key_place = jnp.concatenate(place_list, 0)
        usable = jnp.concatenate(usable_list, 0)
        query_place = jnp.arange(TOK_DEV, dtype=jnp.int32)
        allowed = (key_place[None, :] <= query_place[:, None]) & usable[None, :]
        scores = jnp.einsum('qhd,khd->hqk', query_blk.astype(jnp.float32), key_all.astype(jnp.float32)) * score_scale
        scores = jnp.where(allowed[None], scores, -jnp.inf)
        row_peak = lax.optimization_barrier(jnp.max(scores, axis=-1, keepdims=True))
        exp_scores = jnp.exp(scores - row_peak)
        row_total = lax.optimization_barrier(jnp.sum(exp_scores, axis=-1))
        rounded = lax.optimization_barrier(exp_scores.astype(jnp.bfloat16)).astype(jnp.float32)
        weighted = jnp.einsum('hqk,khd->hqd', rounded, value_all.astype(jnp.float32))
        attention = (weighted / row_total[..., None]).astype(jnp.bfloat16)
        attention = attention.transpose(1, 0, 2).reshape(TOK_DEV, HEADS * head_width)
        mixed = jnp.zeros((TOK_DEV, D), jnp.float32)
        for member in range(N_HEAD):
            partial_sum = jnp.dot(attention[:, member * group_width:(member + 1) * group_width], out_weight[member * group_width:(member + 1) * group_width], preferred_element_type=jnp.float32)
            mixed = mixed + lax.optimization_barrier(partial_sum.astype(jnp.bfloat16)).astype(jnp.float32)
        return mixed.astype(jnp.bfloat16)
    blocks = lax.map(one_block, jnp.arange(N_SEQ, dtype=jnp.int32))
    return blocks.reshape(TOKENS, D)
```

```python
import functools
import math

import jax
import jax.numpy as jnp
from jax import lax
from jax.experimental import pallas as pl
from jax.experimental.pallas import tpu as pltpu
from jax.sharding import PartitionSpec as P

HEAD_DIM = 128
WIN = 512
MED = 4
COARSE = 64
NEG = -1e30
EXP2_SCALE = math.log2(math.e) / math.sqrt(HEAD_DIM)
F32 = jnp.float32
BF16 = jnp.bfloat16


def mm(a, b):
    return lax.dot_general(a, b, (((1,), (0,)), ((), ())), preferred_element_type=F32)


def mm_t(a, b):
    return lax.dot_general(a, b, (((1,), (1,)), ((), ())), preferred_element_type=F32)


def pool_kernel(heads, k_ref, v_ref, mw_ref, cw_ref, med_ref, coarse_ref):
    rows = k_ref.shape[0]
    n_med, n_coarse = rows // MED, rows // COARSE
    med_on = (
        lax.broadcasted_iota(jnp.int32, (n_med, rows), 1) // MED
        == lax.broadcasted_iota(jnp.int32, (n_med, rows), 0)
    )
    coarse_on = (
        lax.broadcasted_iota(jnp.int32, (n_coarse, rows), 1) // COARSE
        == lax.broadcasted_iota(jnp.int32, (n_coarse, rows), 0)
    )

    def pooled(on, w, x):
        spread = jnp.where(on, w, 0.0)
        high = spread.astype(BF16)
        low = (spread - high.astype(F32)).astype(BF16)
        return mm(high, x) + mm(low, x)

    for t, ref in enumerate((k_ref, v_ref)):
        for h in range(heads):
            cols = pl.ds(h * HEAD_DIM, HEAD_DIM)
            at = pl.ds((t * heads + h) * HEAD_DIM, HEAD_DIM)
            x = ref[:, cols]
            row = pl.ds(t * heads + h, 1)
            med_ref[:, at] = pooled(med_on, mw_ref[row, :], x).astype(BF16)
            coarse_ref[:, at] = pooled(coarse_on, cw_ref[row, :], x).astype(BF16)


def pool(keys, values, med_weight, coarse_weight):
    rows, width = keys.shape
    heads = width // HEAD_DIM
    mw = jnp.tile(med_weight.reshape(2 * heads, MED), (1, rows // MED))
    cw = jnp.tile(coarse_weight.reshape(2 * heads, COARSE), (1, rows // COARSE))
    return pl.pallas_call(
        functools.partial(pool_kernel, heads),
        out_shape=(
            jax.ShapeDtypeStruct((rows // MED, 2 * width), BF16),
            jax.ShapeDtypeStruct((rows // COARSE, 2 * width), BF16),
        ),
        compiler_params=pltpu.CompilerParams(vmem_limit_bytes=32 << 20),
        cost_estimate=pl.CostEstimate(
            flops=4 * 136 * rows * 2 * width, bytes_accessed=3 << 20, transcendentals=0
        ),
        name="pool",
    )(keys, values, mw, cw)


def near_kernel(tile, pos_ref, q_ref, k_ref, v_ref, ek_ref, ev_ref, acc_ref, stat_ref):
    rows = q_ref.shape[0]
    has_edge = pos_ref[0] >= 1
    lane = lax.broadcasted_iota(jnp.int32, (tile, 128), 1)
    on_diag = lax.broadcasted_iota(jnp.int32, (tile, tile), 1) <= lax.broadcasted_iota(
        jnp.int32, (tile, tile), 0
    )
    for i in range(rows // tile):
        at = pl.ds(i * tile, tile)
        q = q_ref[at, :]
        diag = jnp.where(on_diag, mm_t(q, k_ref[at, :]), NEG)
        edge = jnp.where(has_edge, mm_t(q, ek_ref[...]), NEG)
        peak = jnp.maximum(
            jnp.max(diag, axis=1, keepdims=True), jnp.max(edge, axis=1, keepdims=True)
        )
        if i:
            past = mm_t(q, k_ref[: i * tile, :])
            peak = jnp.maximum(peak, jnp.max(past, axis=1, keepdims=True))
        p = jnp.exp2((diag - peak) * EXP2_SCALE)
        total = jnp.sum(p, axis=1, keepdims=True)
        acc = mm(p.astype(BF16), v_ref[at, :])
        p = jnp.exp2((edge - peak) * EXP2_SCALE)
        total += jnp.sum(p, axis=1, keepdims=True)
        acc += mm(p.astype(BF16), ev_ref[...])
        if i:
            p = jnp.exp2((past - peak) * EXP2_SCALE)
            total += jnp.sum(p, axis=1, keepdims=True)
            acc += mm(p.astype(BF16), v_ref[: i * tile, :])
        acc_ref[at, :] = acc
        stat_ref[0, at, :] = jnp.where(lane == 0, peak, total)


def near(position, queries, keys, values, edge_keys, edge_values):
    rows, width = queries.shape
    heads = width // HEAD_DIM
    col = pl.BlockSpec((rows, HEAD_DIM), lambda h, *_: (0, h))
    return pl.pallas_call(
        functools.partial(near_kernel, 256),
        out_shape=(
            jax.ShapeDtypeStruct((rows, width), F32),
            jax.ShapeDtypeStruct((heads, rows, 128), F32),
        ),
        grid_spec=pltpu.PrefetchScalarGridSpec(
            num_scalar_prefetch=1,
            grid=(heads,),
            in_specs=[col] * 5,
            out_specs=(col, pl.BlockSpec((1, rows, 128), lambda h, *_: (h, 0, 0))),
        ),
        compiler_params=pltpu.CompilerParams(vmem_limit_bytes=32 << 20),
        cost_estimate=pl.CostEstimate(
            flops=4 * rows * 2 * rows * width, bytes_accessed=9 << 20, transcendentals=0
        ),
        name="near",
    )(position, queries, keys, values, edge_keys, edge_values)


def far_kernel(
    tile, per_coarse, pos_ref, q_ref, m2k, m2v, m3k, m3v, m4k, m4v, ck, cv, acc_ref, stat_ref, out_ref
):
    rows = q_ref.shape[0]
    pos = pos_ref[0]
    n_coarse = ck.shape[0]
    usable = lax.broadcasted_iota(jnp.int32, (1, n_coarse), 1) < pos * per_coarse
    for i in range(rows // tile):
        at = pl.ds(i * tile, tile)
        q = q_ref[at, :]
        parts = []
        for distance, k in ((2, m2k), (3, m3k), (4, m4k)):
            parts.append(jnp.where(pos >= distance, mm_t(q, k[...]), NEG))
        parts.append(jnp.where(usable, mm_t(q, ck[...]), NEG))
        stat = stat_ref[0, at, :]
        near_peak, near_total = stat[:, 0:1], stat[:, 1:2]
        peak = near_peak
        for s in parts:
            peak = jnp.maximum(peak, jnp.max(s, axis=1, keepdims=True))
        shrink = jnp.exp2((near_peak - peak) * EXP2_SCALE)
        total = near_total * shrink
        acc = acc_ref[at, :] * shrink
        for s, v in zip(parts, (m2v, m3v, m4v, cv)):
            p = jnp.exp2((s - peak) * EXP2_SCALE)
            total += jnp.sum(p, axis=1, keepdims=True)
            acc += mm(p.astype(BF16), v[...])
        out_ref[at, :] = (acc / total).astype(BF16)


def far(position, queries, meds, coarse, acc, stat, chunk, chunks):
    rows, width = queries.shape
    heads = width // HEAD_DIM
    part = rows // chunks
    n_med, n_coarse = meds[0].shape[0], coarse.shape[0]
    col = pl.BlockSpec((part, HEAD_DIM), lambda h, *_: (chunk, h))
    summary = []
    operands = []
    for x, n in ((meds[0], n_med), (meds[1], n_med), (meds[2], n_med), (coarse, n_coarse)):
        summary.append(pl.BlockSpec((n, HEAD_DIM), lambda h, *_: (0, h)))
        summary.append(pl.BlockSpec((n, HEAD_DIM), lambda h, *_: (0, heads + h)))
        operands += [x, x]
    return pl.pallas_call(
        functools.partial(far_kernel, part, rows // COARSE),
        out_shape=jax.ShapeDtypeStruct((part, width), BF16),
        grid_spec=pltpu.PrefetchScalarGridSpec(
            num_scalar_prefetch=1,
            grid=(heads,),
            in_specs=[col]
            + summary
            + [col, pl.BlockSpec((1, part, 128), lambda h, *_: (h, chunk, 0))],
            out_specs=pl.BlockSpec((part, HEAD_DIM), lambda h, *_: (0, h)),
        ),
        compiler_params=pltpu.CompilerParams(vmem_limit_bytes=32 << 20),
        cost_estimate=pl.CostEstimate(
            flops=4 * part * (3 * n_med + n_coarse) * width,
            bytes_accessed=6 << 20,
            transcendentals=0,
        ),
        name="far",
    )(position, queries, *operands, acc, stat)


def project_kernel(members, head_ref, a_ref, w_ref, *outs):
    for k in range(members):

        @pl.when(pl.program_id(0) == k)
        def _():
            outs[k][...] = mm(a_ref[...], w_ref[...]).astype(BF16)


def project(head, attention, weight, members):
    rows, depth = attention.shape
    width = weight.shape[1] // members
    whole = pl.BlockSpec((rows, width), lambda k, *_: (0, 0))
    return pl.pallas_call(
        functools.partial(project_kernel, members),
        out_shape=[jax.ShapeDtypeStruct((rows, width), BF16)] * members,
        grid_spec=pltpu.PrefetchScalarGridSpec(
            num_scalar_prefetch=1,
            grid=(members,),
            in_specs=[
                pl.BlockSpec((rows, depth), lambda k, *_: (0, 0)),
                pl.BlockSpec((depth, width), lambda k, head: (0, (head[0] + k) % members)),
            ],
            out_specs=[whole] * members,
        ),
        compiler_params=pltpu.CompilerParams(vmem_limit_bytes=32 << 20),
        cost_estimate=pl.CostEstimate(
            flops=2 * rows * depth * width * members,
            bytes_accessed=2 * depth * width * members,
            transcendentals=0,
        ),
        name="project",
    )(head, attention, weight)


def shifted(block, axis, distance):
    devices = range(lax.axis_size(axis))
    return lax.ppermute(
        block, axis, [(i - distance, i) for i in devices if i - distance in devices]
    )


def body(queries, keys, values, med_weight, coarse_weight, out_weight):
    n_seq = lax.axis_size("seq")
    members = lax.axis_size("head")
    position = lax.axis_index("seq")
    pos = position.astype(jnp.int32).reshape(1)
    head = lax.axis_index("head").astype(jnp.int32).reshape(1)

    med, coarse = pool(keys, values, med_weight, coarse_weight)
    inner = 8
    groups = [[a * inner + b for b in range(inner)] for a in range(n_seq // inner)]
    across = [[a * inner + b for a in range(n_seq // inner)] for b in range(inner)]
    near_coarse = lax.all_gather(coarse, "seq", axis=0, tiled=True, axis_index_groups=groups)
    all_coarse = lax.all_gather(near_coarse, "seq", axis=0, tiled=True, axis_index_groups=across)

    edge_keys = shifted(keys, "seq", 1)
    edge_values = shifted(values, "seq", 1)
    med2 = shifted(med, "seq", 2)
    med4 = shifted(med, "seq", 4)
    other = jnp.where(position % 2 == 0, med2, med4)
    med3 = lax.ppermute(other, "seq", [(i, i ^ 1) for i in range(n_seq)])

    acc, stat = near(pos, queries, keys, values, edge_keys, edge_values)
    chunks = 2
    pieces = []
    for c in range(chunks):
        attention = far(pos, queries, (med2, med3, med4), all_coarse, acc, stat, c, chunks)
        partial = project(head, attention, out_weight, members)
        total = partial[0].astype(F32)
        for k in (2, 1, 3):
            got = lax.ppermute(
                partial[k], "head", [(i, (i + k) % members) for i in range(members)]
            )
            total = total + got.astype(F32)
        pieces.append(total.astype(BF16))
    return jnp.concatenate(pieces, axis=0)


def solution(mesh):
    placed = (
        P("seq", "head"),
        P("seq", "head"),
        P("seq", "head"),
        P(None, "head", None),
        P(None, "head", None),
        P("head", None),
    )
    return jax.shard_map(
        body, mesh=mesh, in_specs=placed, out_specs=P("seq", "head"), check_vma=False
    )
```

```python
import functools
import math

import jax
import jax.numpy as jnp
from jax import lax
from jax.experimental import pallas as pl
from jax.experimental.pallas import tpu as pltpu
from jax.sharding import PartitionSpec as P

HEAD_DIM = 128
WIN = 512
MED = 4
COARSE = 64
CHIPS_X = 4
PLANE = 2 * CHIPS_X
PLANES = 8
NEG = -1e30
EXP2_SCALE = math.log2(math.e) / math.sqrt(HEAD_DIM)
F32 = jnp.float32
BF16 = jnp.bfloat16


def mm(a, b):
    return lax.dot_general(a, b, (((1,), (0,)), ((), ())), preferred_element_type=F32)


def mm_t(a, b):
    return lax.dot_general(a, b, (((1,), (1,)), ((), ())), preferred_element_type=F32)


def pool_kernel(heads, k_ref, v_ref, mw_ref, cw_ref, med_ref, coarse_ref):
    rows = k_ref.shape[0]
    n_med, n_coarse = rows // MED, rows // COARSE
    med_on = (
        lax.broadcasted_iota(jnp.int32, (n_med, rows), 1) // MED
        == lax.broadcasted_iota(jnp.int32, (n_med, rows), 0)
    )
    coarse_on = (
        lax.broadcasted_iota(jnp.int32, (n_coarse, rows), 1) // COARSE
        == lax.broadcasted_iota(jnp.int32, (n_coarse, rows), 0)
    )

    def pooled(on, w, x):
        spread = jnp.where(on, w, 0.0)
        high = spread.astype(BF16)
        low = (spread - high.astype(F32)).astype(BF16)
        return mm(high, x) + mm(low, x)

    for t, ref in enumerate((k_ref, v_ref)):
        for h in range(heads):
            cols = pl.ds(h * HEAD_DIM, HEAD_DIM)
            at = pl.ds((t * heads + h) * HEAD_DIM, HEAD_DIM)
            x = ref[:, cols]
            row = pl.ds(t * heads + h, 1)
            med_ref[:, at] = pooled(med_on, mw_ref[row, :], x).astype(BF16)
            coarse_ref[:, at] = pooled(coarse_on, cw_ref[row, :], x).astype(BF16)


def pool(keys, values, med_weight, coarse_weight):
    rows, width = keys.shape
    heads = width // HEAD_DIM
    mw = jnp.tile(med_weight.reshape(2 * heads, MED), (1, rows // MED))
    cw = jnp.tile(coarse_weight.reshape(2 * heads, COARSE), (1, rows // COARSE))
    return pl.pallas_call(
        functools.partial(pool_kernel, heads),
        out_shape=(
            jax.ShapeDtypeStruct((rows // MED, 2 * width), BF16),
            jax.ShapeDtypeStruct((rows // COARSE, 2 * width), BF16),
        ),
        compiler_params=pltpu.CompilerParams(vmem_limit_bytes=60 << 20),
        cost_estimate=pl.CostEstimate(
            flops=4 * 136 * rows * 2 * width, bytes_accessed=3 << 20, transcendentals=0
        ),
        name="pool",
    )(keys, values, mw, cw)


def near_kernel(tile, pos_ref, q_ref, k_ref, v_ref, ek_ref, ev_ref, acc_ref, stat_ref):
    rows = q_ref.shape[0]
    has_edge = pos_ref[0] >= 1
    lane = lax.broadcasted_iota(jnp.int32, (tile, 128), 1)
    on_diag = lax.broadcasted_iota(jnp.int32, (tile, tile), 1) <= lax.broadcasted_iota(
        jnp.int32, (tile, tile), 0
    )
    for i in range(rows // tile):
        at = pl.ds(i * tile, tile)
        q = q_ref[at, :]
        diag = jnp.where(on_diag, mm_t(q, k_ref[at, :]), NEG)
        edge = jnp.where(has_edge, mm_t(q, ek_ref[...]), NEG)
        peak = jnp.maximum(
            jnp.max(diag, axis=1, keepdims=True), jnp.max(edge, axis=1, keepdims=True)
        )
        if i:
            past = mm_t(q, k_ref[: i * tile, :])
            peak = jnp.maximum(peak, jnp.max(past, axis=1, keepdims=True))
        p = jnp.exp2((diag - peak) * EXP2_SCALE)
        total = jnp.sum(p, axis=1, keepdims=True)
        acc = mm(p.astype(BF16), v_ref[at, :])
        p = jnp.exp2((edge - peak) * EXP2_SCALE)
        total += jnp.sum(p, axis=1, keepdims=True)
        acc += mm(p.astype(BF16), ev_ref[...])
        if i:
            p = jnp.exp2((past - peak) * EXP2_SCALE)
            total += jnp.sum(p, axis=1, keepdims=True)
            acc += mm(p.astype(BF16), v_ref[: i * tile, :])
        acc_ref[at, :] = acc
        stat_ref[0, at, :] = jnp.where(lane == 0, peak, total)


def near(position, queries, keys, values, edge_keys, edge_values):
    rows, width = queries.shape
    heads = width // HEAD_DIM
    col = pl.BlockSpec((rows, HEAD_DIM), lambda h, *_: (0, h))
    return pl.pallas_call(
        functools.partial(near_kernel, 256),
        out_shape=(
            jax.ShapeDtypeStruct((rows, width), F32),
            jax.ShapeDtypeStruct((heads, rows, 128), F32),
        ),
        grid_spec=pltpu.PrefetchScalarGridSpec(
            num_scalar_prefetch=1,
            grid=(heads,),
            in_specs=[col] * 5,
            out_specs=(col, pl.BlockSpec((1, rows, 128), lambda h, *_: (h, 0, 0))),
        ),
        compiler_params=pltpu.CompilerParams(vmem_limit_bytes=60 << 20),
        cost_estimate=pl.CostEstimate(
            flops=4 * rows * 2 * rows * width, bytes_accessed=9 << 20, transcendentals=0
        ),
        name="near",
    )(position, queries, keys, values, edge_keys, edge_values)


def far_kernel(
    tile, per_coarse, pos_ref, q_ref, m2k, m2v, m3k, m3v, m4k, m4v, mine, other, acc_ref, stat_ref, out_ref
):
    rows = q_ref.shape[0]
    pos = pos_ref[0]
    first = pos % 2 == 0
    ck = jnp.where(first, mine[...], other[...])
    cv = jnp.where(first, other[...], mine[...])
    j = lax.broadcasted_iota(jnp.int32, (1, ck.shape[0]), 1)
    pair = 2 * per_coarse
    group = j // (pair * 2 * CHIPS_X)
    step = jnp.where(group == 2, -1, jnp.where(group == 3, 2, group))
    slot = j // (2 * pair) % CHIPS_X
    half = j // pair % 2
    core = j // per_coarse % 2
    z = (pos // PLANE - step - 4 * half) & (PLANES - 1)
    x = (pos % PLANE // 2 - slot) & (CHIPS_X - 1)
    usable = z * PLANE + x * 2 + core < pos
    for i in range(rows // tile):
        at = pl.ds(i * tile, tile)
        q = q_ref[at, :]
        parts = []
        for distance, k in ((2, m2k), (3, m3k), (4, m4k)):
            parts.append(jnp.where(pos >= distance, mm_t(q, k[...]), NEG))
        parts.append(jnp.where(usable, mm_t(q, ck), NEG))
        stat = stat_ref[0, at, :]
        near_peak, near_total = stat[:, 0:1], stat[:, 1:2]
        peak = near_peak
        for s in parts:
            peak = jnp.maximum(peak, jnp.max(s, axis=1, keepdims=True))
        shrink = jnp.exp2((near_peak - peak) * EXP2_SCALE)
        total = near_total * shrink
        acc = acc_ref[at, :] * shrink
        for s, v in zip(parts, (m2v[...], m3v[...], m4v[...], cv)):
            p = jnp.exp2((s - peak) * EXP2_SCALE)
            total += jnp.sum(p, axis=1, keepdims=True)
            acc += mm(p.astype(BF16), v)
        out_ref[at, :] = (acc / total).astype(BF16)


def far(position, queries, meds, mine, other, acc, stat, chunk, chunks):
    rows, width = queries.shape
    heads = width // HEAD_DIM
    part = rows // chunks
    n_med, n_coarse = meds[0].shape[0], mine.shape[0]
    col = pl.BlockSpec((part, HEAD_DIM), lambda h, *_: (chunk, h))
    summary = []
    operands = []
    for x in meds:
        summary.append(pl.BlockSpec((n_med, HEAD_DIM), lambda h, *_: (0, h)))
        summary.append(pl.BlockSpec((n_med, HEAD_DIM), lambda h, *_: (0, heads + h)))
        operands += [x, x]
    for x in (mine, other):
        summary.append(pl.BlockSpec((n_coarse, HEAD_DIM), lambda h, *_: (0, h)))
        operands.append(x)
    return pl.pallas_call(
        functools.partial(far_kernel, part, rows // COARSE),
        out_shape=jax.ShapeDtypeStruct((part, width), BF16),
        grid_spec=pltpu.PrefetchScalarGridSpec(
            num_scalar_prefetch=1,
            grid=(heads,),
            in_specs=[col]
            + summary
            + [col, pl.BlockSpec((1, part, 128), lambda h, *_: (h, chunk, 0))],
            out_specs=pl.BlockSpec((part, HEAD_DIM), lambda h, *_: (0, h)),
        ),
        compiler_params=pltpu.CompilerParams(vmem_limit_bytes=60 << 20),
        cost_estimate=pl.CostEstimate(
            flops=4 * part * (3 * n_med + n_coarse) * width,
            bytes_accessed=6 << 20,
            transcendentals=0,
        ),
        name="far",
    )(position, queries, *operands, acc, stat)


def project_kernel(members, head_ref, a_ref, w_ref, *outs):
    for k in range(members):

        @pl.when(pl.program_id(0) == k)
        def _():
            outs[k][...] = mm(a_ref[...], w_ref[...]).astype(BF16)


def project(head, attention, weight, members):
    rows, depth = attention.shape
    width = weight.shape[1] // members
    whole = pl.BlockSpec((rows, width), lambda k, *_: (0, 0))
    return pl.pallas_call(
        functools.partial(project_kernel, members),
        out_shape=[jax.ShapeDtypeStruct((rows, width), BF16)] * members,
        grid_spec=pltpu.PrefetchScalarGridSpec(
            num_scalar_prefetch=1,
            grid=(members,),
            in_specs=[
                pl.BlockSpec((rows, depth), lambda k, *_: (0, 0)),
                pl.BlockSpec((depth, width), lambda k, head: (0, (head[0] + k) % members)),
            ],
            out_specs=[whole] * members,
        ),
        compiler_params=pltpu.CompilerParams(vmem_limit_bytes=60 << 20),
        cost_estimate=pl.CostEstimate(
            flops=2 * rows * depth * width * members,
            bytes_accessed=2 * depth * width * members,
            transcendentals=0,
        ),
        name="project",
    )(head, attention, weight)


def shifted(block, axis, distance):
    devices = range(lax.axis_size(axis))
    return lax.ppermute(
        block, axis, [(i - distance, i) for i in devices if i - distance in devices]
    )


def body(queries, keys, values, med_weight, coarse_weight, out_weight):
    n_seq = lax.axis_size("seq")
    members = lax.axis_size("head")
    position = lax.axis_index("seq")
    pos = position.astype(jnp.int32).reshape(1)
    head = lax.axis_index("head").astype(jnp.int32).reshape(1)

    med, coarse = pool(keys, values, med_weight, coarse_weight)
    core0 = position % 2 == 0
    swap = [(i, i ^ 1) for i in range(n_seq)]

    def place(z, x, core):
        return z * PLANE + x * 2 + core

    def move(block, dz, dx):
        route = [
            (place(z, x, c), place((z + dz) % PLANES, (x + dx) % CHIPS_X, c))
            for z in range(PLANES)
            for x in range(CHIPS_X)
            for c in range(2)
        ]
        return lax.ppermute(block, "seq", route)

    edge_keys = shifted(keys, "seq", 1)
    edge_values = shifted(values, "seq", 1)

    width = keys.shape[1]
    coarse_k, coarse_v = coarse[:, :width], coarse[:, width:]
    kept = jnp.where(core0, coarse_k, coarse_v)
    swapped = lax.ppermute(jnp.where(core0, coarse_v, coarse_k), "seq", swap)
    pair = jnp.where(
        core0, jnp.concatenate([kept, swapped], 0), jnp.concatenate([swapped, kept], 0)
    )
    quad = jnp.concatenate([pair, move(pair, 4, 0)], 0)
    ring = jnp.concatenate([quad] + [move(quad, 0, d) for d in range(1, CHIPS_X)], 0)

    turned = move(med, 0, -1)
    last = [
        (place(z, x, c), place(z + (x + 1) % CHIPS_X // 2, (x - 1) % CHIPS_X, c))
        for z in range(PLANES)
        for x in range(CHIPS_X)
        for c in range(2)
        if z + (x + 1) % CHIPS_X // 2 < PLANES
    ]
    med4 = lax.ppermute(turned, "seq", last)
    edge_keys, edge_values, ring, med = lax.optimization_barrier(
        (edge_keys, edge_values, ring, med)
    )
    rings = [move(ring, d, 0) for d in (1, -1, 2)]
    med2 = shifted(med, "seq", 2)
    acc, stat = near(pos, queries, keys, values, edge_keys, edge_values)
    rings, med2, med4, acc, stat = lax.optimization_barrier((rings, med2, med4, acc, stat))
    mine = jnp.concatenate([ring] + rings, 0)
    other = lax.ppermute(mine, "seq", swap)
    med3 = lax.ppermute(jnp.where(core0, med2, med4), "seq", swap)
    chunks = 2
    pieces = []
    for c in range(chunks):
        attention = far(pos, queries, (med2, med3, med4), mine, other, acc, stat, c, chunks)
        partial = project(head, attention, out_weight, members)
        total = partial[0].astype(F32)
        for k in (2, 1, 3):
            got = lax.ppermute(
                partial[k], "head", [(i, (i + k) % members) for i in range(members)]
            )
            total = total + got.astype(F32)
        pieces.append(total.astype(BF16))
    return jnp.concatenate(pieces, axis=0)


def solution(mesh):
    placed = (
        P("seq", "head"),
        P("seq", "head"),
        P("seq", "head"),
        P(None, "head", None),
        P(None, "head", None),
        P("head", None),
    )
    return jax.shard_map(
        body, mesh=mesh, in_specs=placed, out_specs=P("seq", "head"), check_vma=False
    )
```

```python
import functools
import math

import jax
import jax.numpy as jnp
from jax import lax
from jax.experimental import pallas as pl
from jax.experimental.pallas import tpu as pltpu
from jax.sharding import PartitionSpec as P

HEAD_DIM = 128
WIN = 512
MED = 4
COARSE = 64
CHIPS_X = 4
PLANE = 2 * CHIPS_X
PLANES = 8
NEG = -1e30
EXP2_SCALE = math.log2(math.e) / math.sqrt(HEAD_DIM)
F32 = jnp.float32
BF16 = jnp.bfloat16
HBM = pl.BlockSpec(memory_space=pltpu.HBM)
VMEM = pl.BlockSpec(memory_space=pltpu.VMEM)
SMEM = pl.BlockSpec(memory_space=pltpu.SMEM)


def in_hbm(x):
    return pltpu.with_memory_space_constraint(x, pltpu.HBM)


def mm(a, b):
    return lax.dot_general(a, b, (((1,), (0,)), ((), ())), preferred_element_type=F32)


def mm_t(a, b):
    return lax.dot_general(a, b, (((1,), (1,)), ((), ())), preferred_element_type=F32)


def head_cols(h):
    return pl.ds(h * HEAD_DIM, HEAD_DIM)


def fetch_heads(pairs, sems, heads):
    copies = []
    for h in range(heads):
        copies.append(
            [
                pltpu.make_async_copy(
                    src.at[:, head_cols(h)], dst.at[:, head_cols(h)], sems.at[t, h]
                )
                for t, (src, dst) in enumerate(pairs)
            ]
        )
        for copy in copies[h]:
            copy.start()
    return copies


def pool_kernel(
    heads, pos_ref, k_hbm, v_hbm, mw_ref, cw_ref, med_ref, kept_ref, sent_ref, k_ref, v_ref, rows_ref, sems
):
    copies = fetch_heads(((k_hbm, k_ref), (v_hbm, v_ref)), sems, heads)
    rows = k_ref.shape[0]
    n_med, n_coarse = rows // MED, rows // COARSE
    lane = lax.broadcasted_iota(jnp.int32, (heads, rows), 1)
    for slot, (ref, ratio) in enumerate(((mw_ref, MED), (cw_ref, COARSE))):
        at = lane % ratio
        for t in range(2):
            w = ref[t]
            spread = jnp.zeros((heads, rows), F32)
            for r in range(ratio):
                spread = jnp.where(at == r, w[:, r : r + 1], spread)
            high = spread.astype(BF16).astype(F32)
            rows_ref[slot, 0, t] = high
            rows_ref[slot, 1, t] = spread - high

    def on(n, ratio):
        source = lax.broadcasted_iota(jnp.int32, (n, rows), 1)
        return source // ratio == lax.broadcasted_iota(jnp.int32, (n, rows), 0)

    med_on, coarse_on = on(n_med, MED), on(n_coarse, COARSE)
    first = pos_ref[0] % 2 == 0
    for h in range(heads):
        for copy in copies[h]:
            copy.wait()
        coarse = []
        for t, ref in enumerate((k_ref, v_ref)):
            row = pl.ds(h, 1)
            left = []
            for part in range(2):
                left.append(jnp.where(med_on, rows_ref[0, part, t, row, :], 0.0))
                left.append(jnp.where(coarse_on, rows_ref[1, part, t, row, :], 0.0))
            r = mm(jnp.concatenate(left, axis=0).astype(BF16), ref[:, head_cols(h)])
            r = r[: n_med + n_coarse] + r[n_med + n_coarse :]
            med_ref[t, :, head_cols(h)] = r[:n_med].astype(BF16)
            coarse.append(r[n_med:])
        kept_ref[:, head_cols(h)] = jnp.where(first, coarse[0], coarse[1]).astype(BF16)
        sent_ref[:, head_cols(h)] = jnp.where(first, coarse[1], coarse[0]).astype(BF16)


def pool(position, keys, values, med_weight, coarse_weight):
    rows, width = keys.shape
    heads = width // HEAD_DIM
    half = jax.ShapeDtypeStruct((rows // COARSE, width), BF16)
    return pl.pallas_call(
        functools.partial(pool_kernel, heads),
        out_shape=(jax.ShapeDtypeStruct((2, rows // MED, width), BF16), half, half),
        in_specs=[SMEM, HBM, HBM, VMEM, VMEM],
        out_specs=(VMEM, VMEM, VMEM),
        scratch_shapes=[
            pltpu.VMEM((rows, width), BF16),
            pltpu.VMEM((rows, width), BF16),
            pltpu.VMEM((2, 2, 2, heads, rows), F32),
            pltpu.SemaphoreType.DMA((2, heads)),
        ],
        compiler_params=pltpu.CompilerParams(vmem_limit_bytes=12 << 20),
        cost_estimate=pl.CostEstimate(
            flops=4 * 136 * rows * 2 * width, bytes_accessed=3 << 20, transcendentals=0
        ),
        name="pool",
    )(
        position,
        in_hbm(keys),
        in_hbm(values),
        med_weight,
        coarse_weight,
    )


def attend_kernel(
    first_row, members, heads, per_coarse,
    pos_ref, head_ref, *refs,
):
    sources, w_hbm, outs = refs[:10], refs[10], refs[11 : 11 + members]
    refs = refs[11 + members :]
    targets, w_ref, att_ref, sems, w_sem = refs[:10], *refs[10:]
    q_ref, k_ref, v_ref, ek_ref, ev_ref, m2, m3, m4, mine, other = targets
    rows, width = att_ref.shape
    n_own = first_row + rows
    spans = [pl.ds(first_row, rows), pl.ds(0, n_own), pl.ds(0, n_own)] + [None] * 7
    groups = heads // 2
    copies = {}

    def start(g):
        cols = pl.ds(g * 2 * HEAD_DIM, 2 * HEAD_DIM)
        copies[g] = []
        for t, (src, dst, span) in enumerate(zip(sources, targets, spans)):
            if len(src.shape) == 3:
                src, dst = src.at[:, :, cols], dst.at[:, :, cols]
            elif span is None:
                src, dst = src.at[:, cols], dst.at[:, cols]
            else:
                src, dst = src.at[span, cols], dst.at[:, cols]
            copies[g].append(pltpu.make_async_copy(src, dst, sems.at[t, g]))
            copies[g][-1].start()

    start(0)
    start(1)
    pos = pos_ref[0]
    n_edge, n_med, n_coarse = ek_ref.shape[0], m2.shape[1], mine.shape[0]
    j = lax.broadcasted_iota(jnp.int32, (1, n_coarse), 1)
    pair = 2 * per_coarse
    group = j // (pair * 2 * CHIPS_X)
    step = jnp.where(group == 2, -1, jnp.where(group == 3, 2, group))
    slot = j // (2 * pair) % CHIPS_X
    half = j // pair % 2
    core = j // per_coarse % 2
    z = (pos // PLANE - step - 4 * half) & (PLANES - 1)
    x = (pos % PLANE // 2 - slot) & (CHIPS_X - 1)
    bias = [
        jnp.where(pos >= d, jnp.zeros((1, n), F32), jnp.full((1, n), NEG, F32))
        for d, n in ((1, n_edge), (2, n_med), (3, n_med), (4, n_med))
    ]
    bias.append(jnp.where(z * PLANE + x * 2 + core < pos, 0.0, NEG))
    bias = jnp.concatenate(bias, axis=1)
    first = pos % 2 == 0
    on_diag = lax.broadcasted_iota(jnp.int32, (rows, rows), 1) <= lax.broadcasted_iota(
        jnp.int32, (rows, rows), 0
    )
    w_copies = []
    for h in range(heads):
        if h % 2 == 0:
            g = h // 2
            for copy in copies[g]:
                copy.wait()
            if g + 2 < groups:
                start(g + 2)
            block = lax.rem(head_ref[0] + g, members)
            cols = pl.ds(pl.multiple_of(block * width, width), width)
            w_copies.append(pltpu.make_async_copy(w_hbm.at[:, cols], w_ref.at[g], w_sem.at[g]))
            w_copies[g].start()
        c = head_cols(h)
        a, b = mine[:, c], other[:, c]
        keys = [k_ref[:, c], ek_ref[:, c]] + [m[0, :, c] for m in (m2, m3, m4)]
        values = [v_ref[:, c], ev_ref[:, c]] + [m[1, :, c] for m in (m2, m3, m4)]
        keys = jnp.concatenate(keys + [jnp.where(first, a, b)], axis=0)
        values = jnp.concatenate(values + [jnp.where(first, b, a)], axis=0)
        s = mm_t(q_ref[:, c], keys)
        parts = [s[:, :first_row]] if first_row else []
        parts.append(jnp.where(on_diag, s[:, first_row:n_own], NEG))
        parts.append(s[:, n_own:] + bias)
        s = jnp.concatenate(parts, axis=1)
        peak = jnp.max(s, axis=1, keepdims=True)
        p = jnp.exp2((s - peak) * EXP2_SCALE).astype(BF16)
        got = mm(p, jnp.concatenate([values, jnp.ones_like(values)], axis=1))
        att_ref[:, c] = (got[:, :HEAD_DIM] / got[:, HEAD_DIM:]).astype(BF16)
    for k in range(members):
        w_copies[k].wait()
        outs[k][...] = mm(att_ref[...], w_ref[k]).astype(BF16)


def attend(position, head, queries, pairs, meds, coarse, weight, first_row, part):
    rows, width = queries.shape
    heads = width // HEAD_DIM
    members = weight.shape[1] // width
    operands = [queries, *pairs, *meds, *coarse]
    shapes = [x.shape for x in operands]
    shapes[:3] = [(part, width)] + [(first_row + part, width)] * 2
    n_keys = sum(shape[-2] for shape in shapes[1::2])
    return pl.pallas_call(
        functools.partial(attend_kernel, first_row, members, heads, rows // COARSE),
        out_shape=[jax.ShapeDtypeStruct((part, width), BF16)] * members,
        in_specs=[SMEM, SMEM] + [HBM] * 11,
        out_specs=[VMEM] * members,
        scratch_shapes=[pltpu.VMEM(shape, BF16) for shape in shapes]
        + [
            pltpu.VMEM((members, width, width), BF16),
            pltpu.VMEM((part, width), BF16),
            pltpu.SemaphoreType.DMA((10, heads // 2)),
            pltpu.SemaphoreType.DMA((members,)),
        ],
        compiler_params=pltpu.CompilerParams(vmem_limit_bytes=40 << 20),
        cost_estimate=pl.CostEstimate(
            flops=8 * part * n_keys * width + 2 * part * width * width * members,
            bytes_accessed=2 * width * width * members,
            transcendentals=0,
        ),
        name="attend",
    )(position, head, *[in_hbm(x) for x in operands[:3]], *operands[3:], in_hbm(weight))


def shifted(block, axis, distance):
    devices = range(lax.axis_size(axis))
    return lax.ppermute(
        block, axis, [(i - distance, i) for i in devices if i - distance in devices]
    )


def body(queries, keys, values, med_weight, coarse_weight, out_weight):
    n_seq = lax.axis_size("seq")
    members = lax.axis_size("head")
    position = lax.axis_index("seq")
    pos = position.astype(jnp.int32).reshape(1)
    head = lax.axis_index("head").astype(jnp.int32).reshape(1)
    core0 = (position & 1) == 0
    swap = [(i, i ^ 1) for i in range(n_seq)]

    def place(z, x, core):
        return z * PLANE + x * 2 + core

    def move(block, dz, dx):
        route = [
            (place(z, x, c), place((z + dz) % PLANES, (x + dx) % CHIPS_X, c))
            for z in range(PLANES)
            for x in range(CHIPS_X)
            for c in range(2)
        ]
        return lax.ppermute(block, "seq", route)

    edge_keys = shifted(keys, "seq", 1)

    med, kept, sent = pool(pos, keys, values, med_weight, coarse_weight)
    swapped = lax.ppermute(sent, "seq", swap)
    pair = jnp.where(
        core0, jnp.concatenate([kept, swapped], 0), jnp.concatenate([swapped, kept], 0)
    )
    quad = jnp.concatenate([pair, move(pair, 4, 0)], 0)
    ring = jnp.concatenate([quad] + [move(quad, 0, d) for d in range(1, CHIPS_X)], 0)

    edge_keys, values, ring, med = lax.optimization_barrier((edge_keys, values, ring, med))
    edge_values = shifted(values, "seq", 1)
    rings = [move(ring, d, 0) for d in (1, -1, 2)]
    turned = move(med, 0, -1)
    edge_values, turned, med = lax.optimization_barrier((edge_values, turned, med))
    med2 = shifted(med, "seq", 2)
    last = [
        (place(z, x, c), place(z + (x + 1) % CHIPS_X // 2, (x - 1) % CHIPS_X, c))
        for z in range(PLANES)
        for x in range(CHIPS_X)
        for c in range(2)
        if z + (x + 1) % CHIPS_X // 2 < PLANES
    ]
    med4 = lax.ppermute(turned, "seq", last)
    mine = jnp.concatenate([ring] + rings, 0)
    other = lax.ppermute(mine, "seq", swap)
    med3 = lax.ppermute(jnp.where(core0, med2, med4), "seq", swap)

    chunks = 2
    part = queries.shape[0] // chunks
    pieces = []
    for c in range(chunks):
        partial = attend(
            pos,
            head,
            queries,
            (keys, values, edge_keys, edge_values),
            (med2, med3, med4),
            (mine, other),
            out_weight,
            c * part,
            part,
        )
        total = partial[0].astype(F32)
        for k in (2, 1, 3):
            got = lax.ppermute(
                partial[k], "head", [(i, (i + k) % members) for i in range(members)]
            )
            total = total + got.astype(F32)
        pieces.append(total.astype(BF16))
    return jnp.concatenate(pieces, axis=0)


def solution(mesh):
    placed = (
        P("seq", "head"),
        P("seq", "head"),
        P("seq", "head"),
        P(None, "head", None),
        P(None, "head", None),
        P("head", None),
    )
    return jax.shard_map(
        body, mesh=mesh, in_specs=placed, out_specs=P("seq", "head"), check_vma=False
    )
```

```python
import functools
import math

import jax
import jax.numpy as jnp
from jax import lax
from jax.experimental import pallas as pl
from jax.experimental.pallas import tpu as pltpu
from jax.sharding import PartitionSpec as P

HEAD_DIM = 128
WIN = 512
MED = 4
COARSE = 64
CHIPS_X = 4
PLANE = 2 * CHIPS_X
PLANES = 8
NEG = -1e30
EXP2_SCALE = math.log2(math.e) / math.sqrt(HEAD_DIM)
F32 = jnp.float32
BF16 = jnp.bfloat16
HBM = pl.BlockSpec(memory_space=pltpu.HBM)
VMEM = pl.BlockSpec(memory_space=pltpu.VMEM)
SMEM = pl.BlockSpec(memory_space=pltpu.SMEM)


def in_hbm(x):
    return pltpu.with_memory_space_constraint(x, pltpu.HBM)


def mm(a, b):
    return lax.dot_general(a, b, (((1,), (0,)), ((), ())), preferred_element_type=F32)


def mm_t(a, b):
    return lax.dot_general(a, b, (((1,), (1,)), ((), ())), preferred_element_type=F32)


def head_cols(h):
    return pl.ds(h * HEAD_DIM, HEAD_DIM)


def fetch_heads(pairs, sems, heads):
    copies = []
    for h in range(heads):
        copies.append(
            [
                pltpu.make_async_copy(
                    src.at[:, head_cols(h)], dst.at[:, head_cols(h)], sems.at[t, h]
                )
                for t, (src, dst) in enumerate(pairs)
            ]
        )
        for copy in copies[h]:
            copy.start()
    return copies


def pool_kernel(
    heads, pos_ref, k_hbm, v_hbm, mw_ref, cw_ref, med_ref, kept_ref, sent_ref, k_ref, v_ref, rows_ref, sems
):
    copies = fetch_heads(((k_hbm, k_ref), (v_hbm, v_ref)), sems, heads)
    rows = k_ref.shape[0]
    n_med, n_coarse = rows // MED, rows // COARSE
    lane = lax.broadcasted_iota(jnp.int32, (heads, rows), 1)
    for slot, (ref, ratio) in enumerate(((mw_ref, MED), (cw_ref, COARSE))):
        at = lane % ratio
        for t in range(2):
            w = ref[t]
            spread = jnp.zeros((heads, rows), F32)
            for r in range(ratio):
                spread = jnp.where(at == r, w[:, r : r + 1], spread)
            high = spread.astype(BF16).astype(F32)
            rows_ref[slot, 0, t] = high
            rows_ref[slot, 1, t] = spread - high

    def on(n, ratio):
        source = lax.broadcasted_iota(jnp.int32, (n, rows), 1)
        return source // ratio == lax.broadcasted_iota(jnp.int32, (n, rows), 0)

    med_on, coarse_on = on(n_med, MED), on(n_coarse, COARSE)
    first = pos_ref[0] % 2 == 0
    for h in range(heads):
        for copy in copies[h]:
            copy.wait()
        coarse = []
        for t, ref in enumerate((k_ref, v_ref)):
            row = pl.ds(h, 1)
            left = []
            for part in range(2):
                left.append(jnp.where(med_on, rows_ref[0, part, t, row, :], 0.0))
                left.append(jnp.where(coarse_on, rows_ref[1, part, t, row, :], 0.0))
            r = mm(jnp.concatenate(left, axis=0).astype(BF16), ref[:, head_cols(h)])
            r = r[: n_med + n_coarse] + r[n_med + n_coarse :]
            med_ref[t, :, head_cols(h)] = r[:n_med].astype(BF16)
            coarse.append(r[n_med:])
        kept_ref[:, head_cols(h)] = jnp.where(first, coarse[0], coarse[1]).astype(BF16)
        sent_ref[:, head_cols(h)] = jnp.where(first, coarse[1], coarse[0]).astype(BF16)


def pool(position, keys, values, med_weight, coarse_weight):
    rows, width = keys.shape
    heads = width // HEAD_DIM
    half = jax.ShapeDtypeStruct((rows // COARSE, width), BF16)
    return pl.pallas_call(
        functools.partial(pool_kernel, heads),
        out_shape=(jax.ShapeDtypeStruct((2, rows // MED, width), BF16), half, half),
        in_specs=[SMEM, HBM, HBM, VMEM, VMEM],
        out_specs=(VMEM, VMEM, VMEM),
        scratch_shapes=[
            pltpu.VMEM((rows, width), BF16),
            pltpu.VMEM((rows, width), BF16),
            pltpu.VMEM((2, 2, 2, heads, rows), F32),
            pltpu.SemaphoreType.DMA((2, heads)),
        ],
        compiler_params=pltpu.CompilerParams(vmem_limit_bytes=12 << 20),
        cost_estimate=pl.CostEstimate(
            flops=4 * 136 * rows * 2 * width, bytes_accessed=3 << 20, transcendentals=0
        ),
        name="pool",
    )(
        position,
        in_hbm(keys),
        in_hbm(values),
        med_weight,
        coarse_weight,
    )


def attend_kernel(
    first_row, members, heads, per_coarse,
    pos_ref, head_ref, *refs,
):
    sources, w_hbm, outs = refs[:10], refs[10], refs[11 : 11 + members]
    refs = refs[11 + members :]
    targets, w_ref, att_ref, sems, w_sem = refs[:10], *refs[10:]
    q_ref, k_ref, v_ref, ek_ref, ev_ref, m2, m3, m4, mine, other = targets
    rows, width = att_ref.shape
    n_own = first_row + rows
    spans = [pl.ds(first_row, rows), pl.ds(0, n_own), pl.ds(0, n_own)] + [None] * 7
    groups = heads // 2
    copies = {}

    def start(g):
        cols = pl.ds(g * 2 * HEAD_DIM, 2 * HEAD_DIM)
        copies[g] = []
        for t, (src, dst, span) in enumerate(zip(sources, targets, spans)):
            if len(src.shape) == 3:
                src, dst = src.at[:, :, cols], dst.at[:, :, cols]
            elif span is None:
                src, dst = src.at[:, cols], dst.at[:, cols]
            else:
                src, dst = src.at[span, cols], dst.at[:, cols]
            copies[g].append(pltpu.make_async_copy(src, dst, sems.at[t, g]))
            copies[g][-1].start()

    start(0)
    start(1)
    pos = pos_ref[0]
    n_edge, n_med, n_coarse = ek_ref.shape[0], m2.shape[1], mine.shape[0]
    j = lax.broadcasted_iota(jnp.int32, (1, n_coarse), 1)
    pair = 2 * per_coarse
    group = j // (pair * 2 * CHIPS_X)
    step = jnp.where(group == 2, -1, jnp.where(group == 3, 2, group))
    slot = j // (2 * pair) % CHIPS_X
    half = j // pair % 2
    core = j // per_coarse % 2
    z = (pos // PLANE - step - 4 * half) & (PLANES - 1)
    x = (pos % PLANE // 2 - slot) & (CHIPS_X - 1)
    bias = [
        jnp.where(pos >= d, jnp.zeros((1, n), F32), jnp.full((1, n), NEG, F32))
        for d, n in ((1, n_edge), (2, n_med), (3, n_med), (4, n_med))
    ]
    bias.append(jnp.where(z * PLANE + x * 2 + core < pos, 0.0, NEG))
    bias = jnp.concatenate(bias, axis=1)
    first = pos % 2 == 0
    on_diag = lax.broadcasted_iota(jnp.int32, (rows, rows), 1) <= lax.broadcasted_iota(
        jnp.int32, (rows, rows), 0
    )
    w_copies = []
    for h in range(heads):
        if h % 2 == 0:
            g = h // 2
            for copy in copies[g]:
                copy.wait()
            if g + 2 < groups:
                start(g + 2)
            block = lax.rem(head_ref[0] + g, members)
            cols = pl.ds(pl.multiple_of(block * width, width), width)
            w_copies.append(pltpu.make_async_copy(w_hbm.at[:, cols], w_ref.at[g], w_sem.at[g]))
            w_copies[g].start()
        c = head_cols(h)
        a, b = mine[:, c], other[:, c]
        keys = [k_ref[:, c], ek_ref[:, c]] + [m[0, :, c] for m in (m2, m3, m4)]
        values = [v_ref[:, c], ev_ref[:, c]] + [m[1, :, c] for m in (m2, m3, m4)]
        keys = jnp.concatenate(keys + [jnp.where(first, a, b)], axis=0)
        values = jnp.concatenate(values + [jnp.where(first, b, a)], axis=0)
        s = mm_t(q_ref[:, c], keys)
        parts = [s[:, :first_row]] if first_row else []
        parts.append(jnp.where(on_diag, s[:, first_row:n_own], NEG))
        parts.append(s[:, n_own:] + bias)
        s = jnp.concatenate(parts, axis=1)
        peak = jnp.max(s, axis=1, keepdims=True)
        p = jnp.exp2((s - peak) * EXP2_SCALE).astype(BF16)
        got = mm(p, jnp.concatenate([values, jnp.ones_like(values)], axis=1))
        att_ref[:, c] = (got[:, :HEAD_DIM] / got[:, HEAD_DIM:]).astype(BF16)
    for k in range(members):
        w_copies[k].wait()
        outs[k][...] = mm(att_ref[...], w_ref[k]).astype(BF16)


def attend(position, head, queries, pairs, meds, coarse, weight, first_row, part):
    rows, width = queries.shape
    heads = width // HEAD_DIM
    members = weight.shape[1] // width
    operands = [queries, *pairs, *meds, *coarse]
    shapes = [x.shape for x in operands]
    shapes[:3] = [(part, width)] + [(first_row + part, width)] * 2
    n_keys = sum(shape[-2] for shape in shapes[1::2])
    return pl.pallas_call(
        functools.partial(attend_kernel, first_row, members, heads, rows // COARSE),
        out_shape=[jax.ShapeDtypeStruct((part, width), BF16)] * members,
        in_specs=[SMEM, SMEM] + [HBM] * 11,
        out_specs=[VMEM] * members,
        scratch_shapes=[pltpu.VMEM(shape, BF16) for shape in shapes]
        + [
            pltpu.VMEM((members, width, width), BF16),
            pltpu.VMEM((part, width), BF16),
            pltpu.SemaphoreType.DMA((10, heads // 2)),
            pltpu.SemaphoreType.DMA((members,)),
        ],
        compiler_params=pltpu.CompilerParams(vmem_limit_bytes=40 << 20),
        cost_estimate=pl.CostEstimate(
            flops=8 * part * n_keys * width + 2 * part * width * width * members,
            bytes_accessed=2 * width * width * members,
            transcendentals=0,
        ),
        name="attend",
    )(position, head, *[in_hbm(x) for x in operands[:3]], *operands[3:], in_hbm(weight))


def shifted(block, axis, distance):
    devices = range(lax.axis_size(axis))
    return lax.ppermute(
        block, axis, [(i - distance, i) for i in devices if i - distance in devices]
    )


def body(queries, keys, values, med_weight, coarse_weight, out_weight):
    n_seq = lax.axis_size("seq")
    members = lax.axis_size("head")
    position = lax.axis_index("seq")
    pos = position.astype(jnp.int32).reshape(1)
    head = lax.axis_index("head").astype(jnp.int32).reshape(1)
    core0 = (position & 1) == 0
    swap = [(i, i ^ 1) for i in range(n_seq)]

    def place(z, x, core):
        return z * PLANE + x * 2 + core

    def move(block, dz, dx):
        route = [
            (place(z, x, c), place((z + dz) % PLANES, (x + dx) % CHIPS_X, c))
            for z in range(PLANES)
            for x in range(CHIPS_X)
            for c in range(2)
        ]
        return lax.ppermute(block, "seq", route)

    width = keys.shape[1]
    edge_keys = shifted(keys, "seq", 1)

    med, kept, sent = pool(pos, keys, values, med_weight, coarse_weight)
    med2 = shifted(med, "seq", 2)
    turned = move(med, 0, -1)
    swapped = lax.ppermute(sent, "seq", swap)
    pair = jnp.where(
        core0, jnp.concatenate([kept, swapped], 0), jnp.concatenate([swapped, kept], 0)
    )
    quad = jnp.concatenate([pair, move(pair, 4, 0)], 0)
    ring = jnp.concatenate([quad] + [move(quad, 0, d) for d in range(1, CHIPS_X)], 0)

    edge_keys, values, ring, turned, med2 = lax.optimization_barrier(
        (edge_keys, values, ring, turned, med2)
    )
    edge_values = shifted(values, "seq", 1)
    rings = [move(ring, d, 0) for d in (1, -1, 2)]
    last = [
        (place(z, x, c), place(z + (x + 1) % CHIPS_X // 2, (x - 1) % CHIPS_X, c))
        for z in range(PLANES)
        for x in range(CHIPS_X)
        for c in range(2)
        if z + (x + 1) % CHIPS_X // 2 < PLANES
    ]
    med4 = lax.ppermute(turned, "seq", last)
    mine = jnp.concatenate([ring] + rings, 0)
    other = lax.ppermute(mine, "seq", swap)
    med3 = lax.ppermute(jnp.where(core0, med2, med4), "seq", swap)

    def send(block, distance):
        return lax.ppermute(
            block, "head", [(i, (i + distance) % members) for i in range(members)]
        )

    chunks = 2
    part = queries.shape[0] // chunks
    pieces = []
    for c in range(chunks):
        own, ahead, across, behind = attend(
            pos,
            head,
            queries,
            (keys, values, edge_keys, edge_values),
            (med2, med3, med4),
            (mine, other),
            out_weight,
            c * part,
            part,
        )
        if c < chunks - 1:
            own, pos = lax.optimization_barrier((own, pos))
            got = [send(across, 2), send(ahead, 1), send(behind, -1)]
        else:
            middle = width // 2
            left = send(across[:, :middle], 1)
            right = send(across[:, middle:], -1)
            ahead = jnp.concatenate(
                [(ahead[:, :middle].astype(F32) + left.astype(F32)).astype(BF16), ahead[:, middle:]], 1
            )
            behind = jnp.concatenate(
                [behind[:, :middle], (behind[:, middle:].astype(F32) + right.astype(F32)).astype(BF16)], 1
            )
            got = [send(ahead, 1), send(behind, -1)]
        total = own.astype(F32)
        for block in got:
            total = total + block.astype(F32)
        pieces.append(total.astype(BF16))
    return jnp.concatenate(pieces, axis=0)


def solution(mesh):
    placed = (
        P("seq", "head"),
        P("seq", "head"),
        P("seq", "head"),
        P(None, "head", None),
        P(None, "head", None),
        P("head", None),
    )
    return jax.shard_map(
        body, mesh=mesh, in_specs=placed, out_specs=P("seq", "head"), check_vma=False
    )
```

```python
import functools
import math

import jax
import jax.numpy as jnp
from jax import lax
from jax.experimental import pallas as pl
from jax.experimental.pallas import tpu as pltpu
from jax.sharding import PartitionSpec as P

HEAD_DIM = 128
WIN = 512
MED = 4
COARSE = 64
CHIPS_X = 4
PLANE = 2 * CHIPS_X
PLANES = 8
FIRST_ROWS = 192
NEG = -1e30
EXP2_SCALE = math.log2(math.e) / math.sqrt(HEAD_DIM)
F32 = jnp.float32
BF16 = jnp.bfloat16
HBM = pl.BlockSpec(memory_space=pltpu.HBM)
VMEM = pl.BlockSpec(memory_space=pltpu.VMEM)
SMEM = pl.BlockSpec(memory_space=pltpu.SMEM)


def in_hbm(x):
    return pltpu.with_memory_space_constraint(x, pltpu.HBM)


def mm(a, b):
    return lax.dot_general(a, b, (((1,), (0,)), ((), ())), preferred_element_type=F32)


def mm_t(a, b):
    return lax.dot_general(a, b, (((1,), (1,)), ((), ())), preferred_element_type=F32)


def head_cols(h):
    return pl.ds(h * HEAD_DIM, HEAD_DIM)


def fetch_heads(pairs, sems, heads):
    copies = []
    for h in range(heads):
        copies.append(
            [
                pltpu.make_async_copy(
                    src.at[:, head_cols(h)], dst.at[:, head_cols(h)], sems.at[t, h]
                )
                for t, (src, dst) in enumerate(pairs)
            ]
        )
        for copy in copies[h]:
            copy.start()
    return copies


def pool_kernel(
    heads,
    pos_ref, k_hbm, v_hbm, mw_ref, cw_hbm,
    med_ref, kept_ref, sent_ref,
    k_ref, v_ref, cw_ref, rows_ref, sems, w_sem,
):
    w_copy = pltpu.make_async_copy(cw_hbm, cw_ref, w_sem.at[0])
    w_copy.start()
    copies = fetch_heads(((k_hbm, k_ref), (v_hbm, v_ref)), sems, heads)
    rows = k_ref.shape[0]
    n_med, n_coarse = rows // MED, rows // COARSE
    lane = lax.broadcasted_iota(jnp.int32, (heads, rows), 1)
    for slot, (ref, ratio) in enumerate(((mw_ref, MED), (cw_ref, COARSE))):
        at = lane % ratio
        if slot:
            w_copy.wait()
        for t in range(2):
            w = ref[t]
            spread = jnp.zeros((heads, rows), F32)
            for r in range(ratio):
                spread = jnp.where(at == r, w[:, r : r + 1], spread)
            high = spread.astype(BF16).astype(F32)
            rows_ref[slot, 0, t] = high
            rows_ref[slot, 1, t] = spread - high

    def on(n, ratio):
        source = lax.broadcasted_iota(jnp.int32, (n, rows), 1)
        return source // ratio == lax.broadcasted_iota(jnp.int32, (n, rows), 0)

    med_on, coarse_on = on(n_med, MED), on(n_coarse, COARSE)
    first = pos_ref[0] % 2 == 0
    for h in range(heads):
        for copy in copies[h]:
            copy.wait()
        coarse = []
        for t, ref in enumerate((k_ref, v_ref)):
            row = pl.ds(h, 1)
            left = []
            for part in range(2):
                left.append(jnp.where(med_on, rows_ref[0, part, t, row, :], 0.0))
                left.append(jnp.where(coarse_on, rows_ref[1, part, t, row, :], 0.0))
            r = mm(jnp.concatenate(left, axis=0).astype(BF16), ref[:, head_cols(h)])
            r = r[: n_med + n_coarse] + r[n_med + n_coarse :]
            med_ref[t, :, head_cols(h)] = r[:n_med].astype(BF16)
            coarse.append(r[n_med:])
        kept_ref[:, head_cols(h)] = jnp.where(first, coarse[0], coarse[1]).astype(BF16)
        sent_ref[:, head_cols(h)] = jnp.where(first, coarse[1], coarse[0]).astype(BF16)


def pool(position, keys, values, med_weight, coarse_weight):
    rows, width = keys.shape
    heads = width // HEAD_DIM
    half = jax.ShapeDtypeStruct((rows // COARSE, width), BF16)
    return pl.pallas_call(
        functools.partial(pool_kernel, heads),
        out_shape=(jax.ShapeDtypeStruct((2, rows // MED, width), BF16), half, half),
        in_specs=[SMEM, HBM, HBM, VMEM, HBM],
        out_specs=(VMEM, VMEM, VMEM),
        scratch_shapes=[
            pltpu.VMEM((rows, width), BF16),
            pltpu.VMEM((rows, width), BF16),
            pltpu.VMEM(coarse_weight.shape, F32),
            pltpu.VMEM((2, 2, 2, heads, rows), F32),
            pltpu.SemaphoreType.DMA((2, heads)),
            pltpu.SemaphoreType.DMA((1,)),
        ],
        compiler_params=pltpu.CompilerParams(vmem_limit_bytes=12 << 20),
        cost_estimate=pl.CostEstimate(
            flops=4 * 136 * rows * 2 * width, bytes_accessed=3 << 20, transcendentals=0
        ),
        name="pool",
    )(
        position,
        in_hbm(keys),
        in_hbm(values),
        med_weight,
        in_hbm(coarse_weight),
    )


def attend_kernel(
    first_row, members, heads, per_coarse,
    pos_ref, head_ref, *refs,
):
    sources, w_hbm, outs = refs[:10], refs[10], refs[11 : 11 + members]
    q_ref, k_ref, v_ref, w_ref, att_ref, sems, w_sem = refs[11 + members :]
    q, k, v, ek, ev, m2, m3, m4, mine, other = sources
    rows, width = att_ref.shape
    n_own = first_row + rows
    n_edge, n_med, n_coarse = ek.shape[0], m2.shape[1], mine.shape[0]
    first = pos_ref[0] % 2 == 0
    n = n_own + n_edge
    moves = [(q, q_ref, first_row, 0, rows)]
    moves += [(k, k_ref, 0, 0, n_own), (v, v_ref, 0, 0, n_own)]
    moves += [(ek, k_ref, 0, n_own, n_edge), (ev, v_ref, 0, n_own, n_edge)]
    for m in (m2, m3, m4):
        moves += [(m.at[0], k_ref, 0, n, n_med), (m.at[1], v_ref, 0, n, n_med)]
        n += n_med
    groups = heads // 2

    def copy(g, t, src, dst, at, to, size):
        cols = pl.ds(g * 2 * HEAD_DIM, 2 * HEAD_DIM)
        return pltpu.make_async_copy(
            src.at[pl.ds(at, size), cols], dst.at[pl.ds(to, size), cols], sems.at[t, g]
        )

    def summaries(g, kv):
        return [copy(g, len(moves) + i, src, dst, 0, n, n_coarse) for i, (src, dst) in enumerate(kv)]

    def start(g):
        for t, args in enumerate(moves):
            copy(g, t, *args).start()

        @pl.when(first)
        def _():
            for c in summaries(g, ((mine, k_ref), (other, v_ref))):
                c.start()

        @pl.when(jnp.logical_not(first))
        def _():
            for c in summaries(g, ((other, k_ref), (mine, v_ref))):
                c.start()

    def finish(g):
        for t, args in enumerate(moves):
            copy(g, t, *args).wait()
        for c in summaries(g, ((mine, k_ref), (other, v_ref))):
            c.wait()

    start(0)
    start(1)
    pos = pos_ref[0]
    j = lax.broadcasted_iota(jnp.int32, (1, n_coarse), 1)
    pair = 2 * per_coarse
    group = j // (pair * 2 * CHIPS_X)
    step = jnp.where(group == 3, 1, jnp.where(group > 0, group - 3, 0))
    slot = j // (2 * pair) % CHIPS_X
    half = j // pair % 2
    core = j // per_coarse % 2
    z = (pos // PLANE - step - 4 * half) & (PLANES - 1)
    x = (pos % PLANE // 2 + slot) & (CHIPS_X - 1)
    bias = [
        jnp.where(pos >= d, jnp.zeros((1, size), F32), jnp.full((1, size), NEG, F32))
        for d, size in ((1, n_edge), (2, n_med), (3, n_med), (4, n_med))
    ]
    bias.append(jnp.where(z * PLANE + x * 2 + core < pos, 0.0, NEG))
    bias = jnp.concatenate(bias, axis=1)
    on_diag = lax.broadcasted_iota(jnp.int32, (rows, rows), 1) <= lax.broadcasted_iota(
        jnp.int32, (rows, rows), 0
    )
    w_copies = []
    for h in range(heads):
        if h % 2 == 0:
            g = h // 2
            finish(g)
            if g + 2 < groups:
                start(g + 2)
            block = lax.rem(head_ref[0] + g, members)
            cols = pl.ds(pl.multiple_of(block * width, width), width)
            w_copies.append(pltpu.make_async_copy(w_hbm.at[:, cols], w_ref.at[g], w_sem.at[g]))
            w_copies[g].start()
        c = head_cols(h)
        s = mm_t(q_ref[:, c], k_ref[:, c])
        parts = [s[:, :first_row]] if first_row else []
        parts.append(jnp.where(on_diag, s[:, first_row:n_own], NEG))
        parts.append(s[:, n_own:] + bias)
        s = jnp.concatenate(parts, axis=1)
        peak = jnp.max(s, axis=1, keepdims=True)
        p = jnp.exp2((s - peak) * EXP2_SCALE).astype(BF16)
        values = v_ref[:, c]
        got = mm(p, jnp.concatenate([values, jnp.ones_like(values)], axis=1))
        att_ref[:, c] = (got[:, :HEAD_DIM] / got[:, HEAD_DIM:]).astype(BF16)
    for k in range(members):
        w_copies[k].wait()
        outs[k][...] = mm(att_ref[...], w_ref[k]).astype(BF16)


def attend(position, head, queries, pairs, meds, coarse, weight, first_row, part):
    rows, width = queries.shape
    heads = width // HEAD_DIM
    members = weight.shape[1] // width
    operands = [queries, *pairs, *meds, *coarse]
    n_keys = first_row + part + pairs[2].shape[0] + 3 * meds[0].shape[1] + coarse[0].shape[0]
    return pl.pallas_call(
        functools.partial(attend_kernel, first_row, members, heads, rows // COARSE),
        out_shape=[jax.ShapeDtypeStruct((part, width), BF16)] * members,
        in_specs=[SMEM, SMEM] + [HBM] * 11,
        out_specs=[VMEM] * members,
        scratch_shapes=[
            pltpu.VMEM((part, width), BF16),
            pltpu.VMEM((n_keys, width), BF16),
            pltpu.VMEM((n_keys, width), BF16),
            pltpu.VMEM((members, width, width), BF16),
            pltpu.VMEM((part, width), BF16),
            pltpu.SemaphoreType.DMA((13, heads // 2)),
            pltpu.SemaphoreType.DMA((members,)),
        ],
        compiler_params=pltpu.CompilerParams(vmem_limit_bytes=40 << 20),
        cost_estimate=pl.CostEstimate(
            flops=part * n_keys * width,
            bytes_accessed=2 * width * width,
            transcendentals=0,
        ),
        name="attend",
    )(position, head, *[in_hbm(x) for x in operands[:3]], *operands[3:], in_hbm(weight))


def shifted(block, axis, distance):
    devices = range(lax.axis_size(axis))
    return lax.ppermute(
        block, axis, [(i - distance, i) for i in devices if i - distance in devices]
    )


def body(queries, keys, values, med_weight, coarse_weight, out_weight):
    n_seq = lax.axis_size("seq")
    members = lax.axis_size("head")
    position = lax.axis_index("seq")
    pos = position.astype(jnp.int32).reshape(1)
    head = lax.axis_index("head").astype(jnp.int32).reshape(1)
    core0 = (position & 1) == 0
    swap = [(i, i ^ 1) for i in range(n_seq)]

    def place(z, x, core):
        return z * PLANE + x * 2 + core

    def move(block, dz, dx):
        route = [
            (place(z, x, c), place((z + dz) % PLANES, (x + dx) % CHIPS_X, c))
            for z in range(PLANES)
            for x in range(CHIPS_X)
            for c in range(2)
        ]
        return lax.ppermute(block, "seq", route)

    width = keys.shape[1]
    edge_keys = shifted(keys, "seq", 1)

    med, kept, sent = pool(pos, keys, values, med_weight, coarse_weight)
    med2 = shifted(med, "seq", 2)
    med4 = shifted(med, "seq", 4)
    swapped = lax.ppermute(sent, "seq", swap)
    pair = jnp.where(
        core0, jnp.concatenate([kept, swapped], 0), jnp.concatenate([swapped, kept], 0)
    )
    quads = [jnp.concatenate([pair, move(pair, 4, 0)], 0)]
    for _ in range(1, CHIPS_X):
        quads.append(move(quads[-1], 0, -1))
    ring = jnp.concatenate(quads, 0)

    edge_keys, values, ring, med2, med4 = lax.optimization_barrier(
        (edge_keys, values, ring, med2, med4)
    )
    edge_values = shifted(values, "seq", 1)
    rings = [move(ring, d, 0) for d in (-2, -1, 1)]
    mine = jnp.concatenate([ring] + rings, 0)
    other = lax.ppermute(mine, "seq", swap)
    med3 = lax.ppermute(jnp.where(core0, med2, med4), "seq", swap)

    def send(block, distance):
        return lax.ppermute(
            block, "head", [(i, (i + distance) % members) for i in range(members)]
        )

    def attend_rows(position, first_row, rows):
        return attend(
            position,
            head,
            queries,
            (keys, values, edge_keys, edge_values),
            (med2, med3, med4),
            (mine, other),
            out_weight,
            first_row,
            rows,
        )

    def total(blocks):
        return functools.reduce(jnp.add, [b.astype(F32) for b in blocks]).astype(BF16)

    split = FIRST_ROWS
    own, ahead, across, behind = attend_rows(pos, 0, split)
    own, pos = lax.optimization_barrier((own, pos))
    first = total([own, send(across, 2), send(ahead, 1), send(behind, -1)])
    own, ahead, across, behind = attend_rows(pos, split, queries.shape[0] - split)
    first, across = lax.optimization_barrier((first, across))
    middle = width // 2
    left = send(across[:, :middle], 1)
    right = send(across[:, middle:], -1)
    ahead = jnp.concatenate([total([ahead[:, :middle], left]), ahead[:, middle:]], 1)
    behind = jnp.concatenate([behind[:, :middle], total([behind[:, middle:], right])], 1)
    second = total([own, send(ahead, 1), send(behind, -1)])
    return jnp.concatenate([first, second], axis=0)


def solution(mesh):
    placed = (
        P("seq", "head"),
        P("seq", "head"),
        P("seq", "head"),
        P(None, "head", None),
        P(None, "head", None),
        P("head", None),
    )
    return jax.shard_map(
        body, mesh=mesh, in_specs=placed, out_specs=P("seq", "head"), check_vma=False
    )
```

```python
import functools
import math

import jax
import jax.numpy as jnp
from jax import lax
from jax.experimental import pallas as pl
from jax.experimental.pallas import tpu as pltpu
from jax.sharding import PartitionSpec as P

HEAD_DIM = 128
WIN = 512
MED = 4
COARSE = 64
CHIPS_X = 4
PLANE = 2 * CHIPS_X
PLANES = 8
ROWS = (128, 160, 224)
NEG = -1e30
EXP2_SCALE = math.log2(math.e) / math.sqrt(HEAD_DIM)
F32 = jnp.float32
BF16 = jnp.bfloat16
HBM = pl.BlockSpec(memory_space=pltpu.HBM)
VMEM = pl.BlockSpec(memory_space=pltpu.VMEM)
SMEM = pl.BlockSpec(memory_space=pltpu.SMEM)


def in_hbm(x):
    return pltpu.with_memory_space_constraint(x, pltpu.HBM)


def mm(a, b):
    return lax.dot_general(a, b, (((1,), (0,)), ((), ())), preferred_element_type=F32)


def mm_t(a, b):
    return lax.dot_general(a, b, (((1,), (1,)), ((), ())), preferred_element_type=F32)


def head_cols(h):
    return pl.ds(h * HEAD_DIM, HEAD_DIM)


def fetch_heads(pairs, sems, heads):
    copies = []
    for h in range(heads):
        copies.append(
            [
                pltpu.make_async_copy(
                    src.at[:, head_cols(h)], dst.at[:, head_cols(h)], sems.at[t, h]
                )
                for t, (src, dst) in enumerate(pairs)
            ]
        )
        for copy in copies[h]:
            copy.start()
    return copies


def pool_kernel(
    heads,
    pos_ref, k_hbm, v_hbm, mw_ref, cw_hbm,
    med_ref, kept_ref, sent_ref,
    k_ref, v_ref, cw_ref, rows_ref, sems, w_sem,
):
    w_copy = pltpu.make_async_copy(cw_hbm, cw_ref, w_sem.at[0])
    w_copy.start()
    copies = fetch_heads(((k_hbm, k_ref), (v_hbm, v_ref)), sems, heads)
    rows = k_ref.shape[0]
    n_med, n_coarse = rows // MED, rows // COARSE
    lane = lax.broadcasted_iota(jnp.int32, (heads, rows), 1)
    for slot, (ref, ratio) in enumerate(((mw_ref, MED), (cw_ref, COARSE))):
        at = lane % ratio
        if slot:
            w_copy.wait()
        for t in range(2):
            w = ref[t]
            spread = jnp.zeros((heads, rows), F32)
            for r in range(ratio):
                spread = jnp.where(at == r, w[:, r : r + 1], spread)
            high = spread.astype(BF16).astype(F32)
            rows_ref[slot, 0, t] = high
            rows_ref[slot, 1, t] = spread - high

    def on(n, ratio):
        source = lax.broadcasted_iota(jnp.int32, (n, rows), 1)
        return source // ratio == lax.broadcasted_iota(jnp.int32, (n, rows), 0)

    med_on, coarse_on = on(n_med, MED), on(n_coarse, COARSE)
    first = pos_ref[0] % 2 == 0
    for h in range(heads):
        for copy in copies[h]:
            copy.wait()
        coarse = []
        for t, ref in enumerate((k_ref, v_ref)):
            row = pl.ds(h, 1)
            left = []
            for part in range(2):
                left.append(jnp.where(med_on, rows_ref[0, part, t, row, :], 0.0))
                left.append(jnp.where(coarse_on, rows_ref[1, part, t, row, :], 0.0))
            r = mm(jnp.concatenate(left, axis=0).astype(BF16), ref[:, head_cols(h)])
            r = r[: n_med + n_coarse] + r[n_med + n_coarse :]
            med_ref[t, :, head_cols(h)] = r[:n_med].astype(BF16)
            coarse.append(r[n_med:])
        kept_ref[:, head_cols(h)] = jnp.where(first, coarse[0], coarse[1]).astype(BF16)
        sent_ref[:, head_cols(h)] = jnp.where(first, coarse[1], coarse[0]).astype(BF16)


def pool(position, keys, values, med_weight, coarse_weight):
    rows, width = keys.shape
    heads = width // HEAD_DIM
    half = jax.ShapeDtypeStruct((rows // COARSE, width), BF16)
    return pl.pallas_call(
        functools.partial(pool_kernel, heads),
        out_shape=(jax.ShapeDtypeStruct((2, rows // MED, width), BF16), half, half),
        in_specs=[SMEM, HBM, HBM, VMEM, HBM],
        out_specs=(VMEM, VMEM, VMEM),
        scratch_shapes=[
            pltpu.VMEM((rows, width), BF16),
            pltpu.VMEM((rows, width), BF16),
            pltpu.VMEM(coarse_weight.shape, F32),
            pltpu.VMEM((2, 2, 2, heads, rows), F32),
            pltpu.SemaphoreType.DMA((2, heads)),
            pltpu.SemaphoreType.DMA((1,)),
        ],
        compiler_params=pltpu.CompilerParams(vmem_limit_bytes=12 << 20),
        cost_estimate=pl.CostEstimate(
            flops=4 * 136 * rows * 2 * width, bytes_accessed=3 << 20, transcendentals=0
        ),
        name="pool",
    )(
        position,
        in_hbm(keys),
        in_hbm(values),
        med_weight,
        in_hbm(coarse_weight),
    )


def attend_kernel(
    first_row, members, heads, per_coarse,
    pos_ref, head_ref, *refs,
):
    sources, w_hbm, outs = refs[:10], refs[10], refs[11 : 11 + members]
    q_ref, k_ref, v_ref, w_ref, att_ref, sems, w_sem = refs[11 + members :]
    q, k, v, ek, ev, m2, m3, m4, mine, other = sources
    rows, width = att_ref.shape
    n_own = first_row + rows
    n_edge, n_med, n_coarse = ek.shape[0], m2.shape[1], mine.shape[0]
    first = pos_ref[0] % 2 == 0
    n = n_own + n_edge
    moves = [(q, q_ref, first_row, 0, rows)]
    moves += [(k, k_ref, 0, 0, n_own), (v, v_ref, 0, 0, n_own)]
    moves += [(ek, k_ref, 0, n_own, n_edge), (ev, v_ref, 0, n_own, n_edge)]
    for m in (m2, m3, m4):
        moves += [(m.at[0], k_ref, 0, n, n_med), (m.at[1], v_ref, 0, n, n_med)]
        n += n_med
    groups = heads // 2

    def copy(g, t, src, dst, at, to, size):
        cols = pl.ds(g * 2 * HEAD_DIM, 2 * HEAD_DIM)
        return pltpu.make_async_copy(
            src.at[pl.ds(at, size), cols], dst.at[pl.ds(to, size), cols], sems.at[t, g]
        )

    def summaries(g, kv):
        return [copy(g, len(moves) + i, src, dst, 0, n, n_coarse) for i, (src, dst) in enumerate(kv)]

    def start(g):
        for t, args in enumerate(moves):
            copy(g, t, *args).start()

        @pl.when(first)
        def _():
            for c in summaries(g, ((mine, k_ref), (other, v_ref))):
                c.start()

        @pl.when(jnp.logical_not(first))
        def _():
            for c in summaries(g, ((other, k_ref), (mine, v_ref))):
                c.start()

    def finish(g):
        for t, args in enumerate(moves):
            copy(g, t, *args).wait()
        for c in summaries(g, ((mine, k_ref), (other, v_ref))):
            c.wait()

    start(0)
    start(1)
    pos = pos_ref[0]
    j = lax.broadcasted_iota(jnp.int32, (1, n_coarse), 1)
    core = j // per_coarse % 2
    j = j // (2 * per_coarse)
    z = (pos // PLANE + 4 * (j % 2) + j // 2 % 2 + 2 * (j // 4 % 2)) & (PLANES - 1)
    group = j // PLANES
    step = jnp.where(group == 3, -1, jnp.where(group > 0, 3 - group, 0))
    x = (pos % PLANE // 2 + step) & (CHIPS_X - 1)
    bias = [
        jnp.where(pos >= d, jnp.zeros((1, size), F32), jnp.full((1, size), NEG, F32))
        for d, size in ((1, n_edge), (2, n_med), (3, n_med), (4, n_med))
    ]
    bias.append(jnp.where(z * PLANE + x * 2 + core < pos, 0.0, NEG))
    bias = jnp.concatenate(bias, axis=1)
    on_diag = lax.broadcasted_iota(jnp.int32, (rows, rows), 1) <= lax.broadcasted_iota(
        jnp.int32, (rows, rows), 0
    )
    w_copies = []
    for h in range(heads):
        if h % 2 == 0:
            g = h // 2
            finish(g)
            if g + 2 < groups:
                start(g + 2)
            block = lax.rem(head_ref[0] + g, members)
            cols = pl.ds(pl.multiple_of(block * width, width), width)
            w_copies.append(pltpu.make_async_copy(w_hbm.at[:, cols], w_ref.at[g], w_sem.at[g]))
            w_copies[g].start()
        c = head_cols(h)
        s = mm_t(q_ref[:, c], k_ref[:, c])
        parts = [s[:, :first_row]] if first_row else []
        parts.append(jnp.where(on_diag, s[:, first_row:n_own], NEG))
        parts.append(s[:, n_own:] + bias)
        s = jnp.concatenate(parts, axis=1)
        peak = jnp.max(s, axis=1, keepdims=True)
        p = jnp.exp2((s - peak) * EXP2_SCALE).astype(BF16)
        values = v_ref[:, c]
        got = mm(p, jnp.concatenate([values, jnp.ones_like(values)], axis=1))
        att_ref[:, c] = (got[:, :HEAD_DIM] / got[:, HEAD_DIM:]).astype(BF16)
    for k in range(members):
        w_copies[k].wait()
        outs[k][...] = mm(att_ref[...], w_ref[k]).astype(BF16)


def attend(position, head, queries, pairs, meds, coarse, weight, first_row, part):
    rows, width = queries.shape
    heads = width // HEAD_DIM
    members = weight.shape[1] // width
    operands = [queries, *pairs, *meds, *coarse]
    n_keys = first_row + part + pairs[2].shape[0] + 3 * meds[0].shape[1] + coarse[0].shape[0]
    return pl.pallas_call(
        functools.partial(attend_kernel, first_row, members, heads, rows // COARSE),
        out_shape=[jax.ShapeDtypeStruct((part, width), BF16)] * members,
        in_specs=[SMEM, SMEM] + [HBM] * 11,
        out_specs=[VMEM] * members,
        scratch_shapes=[
            pltpu.VMEM((part, width), BF16),
            pltpu.VMEM((n_keys, width), BF16),
            pltpu.VMEM((n_keys, width), BF16),
            pltpu.VMEM((members, width, width), BF16),
            pltpu.VMEM((part, width), BF16),
            pltpu.SemaphoreType.DMA((13, heads // 2)),
            pltpu.SemaphoreType.DMA((members,)),
        ],
        compiler_params=pltpu.CompilerParams(vmem_limit_bytes=40 << 20),
        cost_estimate=pl.CostEstimate(
            flops=part * n_keys * width,
            bytes_accessed=2 * width * width,
            transcendentals=0,
        ),
        name="attend",
    )(position, head, *[in_hbm(x) for x in operands[:8]], *operands[8:], in_hbm(weight))


def shifted(block, axis, distance):
    devices = range(lax.axis_size(axis))
    return lax.ppermute(
        block, axis, [(i - distance, i) for i in devices if i - distance in devices]
    )


def body(queries, keys, values, med_weight, coarse_weight, out_weight):
    n_seq = lax.axis_size("seq")
    members = lax.axis_size("head")
    position = lax.axis_index("seq")
    pos = position.astype(jnp.int32).reshape(1)
    head = lax.axis_index("head").astype(jnp.int32).reshape(1)
    core0 = (position & 1) == 0
    swap = [(i, i ^ 1) for i in range(n_seq)]

    def place(z, x, core):
        return z * PLANE + x * 2 + core

    def move(block, dz, dx):
        route = [
            (place(z, x, c), place((z + dz) % PLANES, (x + dx) % CHIPS_X, c))
            for z in range(PLANES)
            for x in range(CHIPS_X)
            for c in range(2)
        ]
        return lax.ppermute(block, "seq", route)

    width = keys.shape[1]
    edge_keys = shifted(keys, "seq", 1)

    med, kept, sent = pool(pos, keys, values, med_weight, coarse_weight)
    med2 = shifted(med, "seq", 2)
    med4 = shifted(med, "seq", 4)
    swapped = lax.ppermute(sent, "seq", swap)
    pair = jnp.where(
        core0, jnp.concatenate([kept, swapped], 0), jnp.concatenate([swapped, kept], 0)
    )
    column = jnp.concatenate([pair, move(pair, 4, 0)], 0)
    for d in (-1, -2):
        column = jnp.concatenate([column, move(column, d, 0)], 0)

    edge_keys, values, column, med2, med4 = lax.optimization_barrier(
        (edge_keys, values, column, med2, med4)
    )
    edge_values = shifted(values, "seq", 1)
    mine = jnp.concatenate([column] + [move(column, 0, d) for d in (-2, -1, 1)], 0)
    other = lax.ppermute(mine, "seq", swap)
    med3 = lax.ppermute(jnp.where(core0, med2, med4), "seq", swap)

    def send(block, distance):
        return lax.ppermute(
            block, "head", [(i, (i + distance) % members) for i in range(members)]
        )

    def attend_rows(position, first_row, rows):
        return attend(
            position,
            head,
            queries,
            (keys, values, edge_keys, edge_values),
            (med2, med3, med4),
            (mine, other),
            out_weight,
            first_row,
            rows,
        )

    def total(blocks):
        return functools.reduce(jnp.add, [b.astype(F32) for b in blocks]).astype(BF16)

    pieces, at = [], 0
    for rows in ROWS:
        own, ahead, across, behind = attend_rows(pos, at, rows)
        own, pos = lax.optimization_barrier((own, pos))
        if pieces:
            pieces[-1], ahead, across, behind = lax.optimization_barrier(
                (pieces[-1], ahead, across, behind)
            )
        pieces.append(total([own, send(across, 2), send(ahead, 1), send(behind, -1)]))
        at += rows
    return jnp.concatenate(pieces, axis=0)


def solution(mesh):
    placed = (
        P("seq", "head"),
        P("seq", "head"),
        P("seq", "head"),
        P(None, "head", None),
        P(None, "head", None),
        P("head", None),
    )
    return jax.shard_map(
        body, mesh=mesh, in_specs=placed, out_specs=P("seq", "head"), check_vma=False
    )
```

```python
import functools
import math

import jax
import jax.numpy as jnp
from jax import lax
from jax.experimental import pallas as pl
from jax.experimental.pallas import tpu as pltpu
from jax.sharding import PartitionSpec as P

HEAD_DIM = 128
WIN = 512
MED = 4
COARSE = 64
CHIPS_X = 4
PLANE = 2 * CHIPS_X
PLANES = 8
NEG = -1e30
EXP2_SCALE = math.log2(math.e) / math.sqrt(HEAD_DIM)
F32 = jnp.float32
BF16 = jnp.bfloat16
HBM = pl.BlockSpec(memory_space=pltpu.HBM)
VMEM = pl.BlockSpec(memory_space=pltpu.VMEM)
SMEM = pl.BlockSpec(memory_space=pltpu.SMEM)


def in_hbm(x):
    return pltpu.with_memory_space_constraint(x, pltpu.HBM)


def mm(a, b):
    return lax.dot_general(a, b, (((1,), (0,)), ((), ())), preferred_element_type=F32)


def mm_t(a, b):
    return lax.dot_general(a, b, (((1,), (1,)), ((), ())), preferred_element_type=F32)


def head_cols(h):
    return pl.ds(h * HEAD_DIM, HEAD_DIM)


def fetch_heads(pairs, sems, heads):
    copies = []
    for h in range(heads):
        copies.append(
            [
                pltpu.make_async_copy(
                    src.at[:, head_cols(h)], dst.at[:, head_cols(h)], sems.at[t, h]
                )
                for t, (src, dst) in enumerate(pairs)
            ]
        )
        for copy in copies[h]:
            copy.start()
    return copies


def pool_kernel(
    heads,
    k_hbm, v_hbm, mw_ref, cw_hbm,
    med_ref, coarse_ref,
    k_ref, v_ref, cw_ref, rows_ref, sems, w_sem,
):
    w_copy = pltpu.make_async_copy(cw_hbm, cw_ref, w_sem.at[0])
    w_copy.start()
    copies = fetch_heads(((k_hbm, k_ref), (v_hbm, v_ref)), sems, heads)
    rows = k_ref.shape[0]
    n_med, n_coarse = rows // MED, rows // COARSE
    lane = lax.broadcasted_iota(jnp.int32, (heads, rows), 1)
    for slot, (ref, ratio) in enumerate(((mw_ref, MED), (cw_ref, COARSE))):
        at = lane % ratio
        if slot:
            w_copy.wait()
        for t in range(2):
            w = ref[t]
            spread = jnp.zeros((heads, rows), F32)
            for r in range(ratio):
                spread = jnp.where(at == r, w[:, r : r + 1], spread)
            high = spread.astype(BF16).astype(F32)
            rows_ref[slot, 0, t] = high
            rows_ref[slot, 1, t] = spread - high

    def on(n, ratio):
        source = lax.broadcasted_iota(jnp.int32, (n, rows), 1)
        return source // ratio == lax.broadcasted_iota(jnp.int32, (n, rows), 0)

    med_on, coarse_on = on(n_med, MED), on(n_coarse, COARSE)
    for h in range(heads):
        for copy in copies[h]:
            copy.wait()
        for t, ref in enumerate((k_ref, v_ref)):
            row = pl.ds(h, 1)
            left = []
            for part in range(2):
                left.append(jnp.where(med_on, rows_ref[0, part, t, row, :], 0.0))
                left.append(jnp.where(coarse_on, rows_ref[1, part, t, row, :], 0.0))
            r = mm(jnp.concatenate(left, axis=0).astype(BF16), ref[:, head_cols(h)])
            r = r[: n_med + n_coarse] + r[n_med + n_coarse :]
            med_ref[t, :, head_cols(h)] = r[:n_med].astype(BF16)
            coarse_ref[:, head_cols(t * heads + h)] = r[n_med:].astype(BF16)


def pool(keys, values, med_weight, coarse_weight):
    rows, width = keys.shape
    heads = width // HEAD_DIM
    return pl.pallas_call(
        functools.partial(pool_kernel, heads),
        out_shape=(jax.ShapeDtypeStruct((2, rows // MED, width), BF16),
            jax.ShapeDtypeStruct((rows // COARSE, 2 * width), BF16),
        ),
        in_specs=[HBM, HBM, VMEM, HBM],
        out_specs=(VMEM, VMEM),
        scratch_shapes=[
            pltpu.VMEM((rows, width), BF16),
            pltpu.VMEM((rows, width), BF16),
            pltpu.VMEM(coarse_weight.shape, F32),
            pltpu.VMEM((2, 2, 2, heads, rows), F32),
            pltpu.SemaphoreType.DMA((2, heads)),
            pltpu.SemaphoreType.DMA((1,)),
        ],
        compiler_params=pltpu.CompilerParams(vmem_limit_bytes=12 << 20),
        cost_estimate=pl.CostEstimate(
            flops=4 * 136 * rows * 2 * width, bytes_accessed=3 << 20, transcendentals=0
        ),
        name="pool",
    )(
        in_hbm(keys),
        in_hbm(values),
        med_weight,
        in_hbm(coarse_weight),
    )


def weigh(scores, peak, values):
    p = jnp.exp2((scores - peak) * EXP2_SCALE).astype(BF16)
    return mm(p, jnp.concatenate([values, jnp.ones_like(values)], axis=1))


def near_kernel(
    tile, heads,
    pos_ref, q_hbm, k_hbm, v_hbm, ek_hbm, ev_hbm,
    acc_ref, peak_ref,
    q_ref, k_ref, v_ref, sems,
):
    rows, n_edge = q_ref.shape[0], ek_hbm.shape[0]
    own, edge = pl.ds(n_edge, rows), pl.ds(0, n_edge)
    copies = fetch_heads(
        (
            (q_hbm, q_ref),
            (k_hbm, k_ref.at[own, :]),
            (v_hbm, v_ref.at[own, :]),
            (ek_hbm, k_ref.at[edge, :]),
            (ev_hbm, v_ref.at[edge, :]),
        ),
        sems,
        heads,
    )
    has_edge = pos_ref[0] >= 1
    on_diag = lax.broadcasted_iota(jnp.int32, (tile, tile), 1) <= lax.broadcasted_iota(
        jnp.int32, (tile, tile), 0
    )
    for h in range(heads):
        for copy in copies[h]:
            copy.wait()
        c = head_cols(h)
        for i in range(rows // tile):
            at, n = pl.ds(i * tile, tile), n_edge + i * tile
            s = mm_t(q_ref[at, c], k_ref[: n + tile, c])
            parts = [jnp.where(has_edge, s[:, :n_edge], NEG)]
            if i:
                parts.append(s[:, n_edge:n])
            parts.append(jnp.where(on_diag, s[:, n:], NEG))
            s = jnp.concatenate(parts, axis=1)
            peak = jnp.max(s, axis=1, keepdims=True)
            acc_ref[at, pl.ds(2 * h * HEAD_DIM, 2 * HEAD_DIM)] = weigh(
                s, peak, v_ref[: n + tile, c]
            )
            peak_ref[at, c] = jnp.broadcast_to(peak, (tile, HEAD_DIM))


def near(position, queries, keys, values, edge_keys, edge_values):
    rows, width = queries.shape
    heads = width // HEAD_DIM
    n_keys = edge_keys.shape[0] + rows
    return pl.pallas_call(
        functools.partial(near_kernel, 256, heads),
        out_shape=(
            jax.ShapeDtypeStruct((rows, 2 * width), F32),
            jax.ShapeDtypeStruct((rows, width), F32),
        ),
        in_specs=[SMEM] + [HBM] * 5,
        out_specs=(VMEM, VMEM),
        scratch_shapes=[
            pltpu.VMEM((rows, width), BF16),
            pltpu.VMEM((n_keys, width), BF16),
            pltpu.VMEM((n_keys, width), BF16),
            pltpu.SemaphoreType.DMA((5, heads)),
        ],
        compiler_params=pltpu.CompilerParams(vmem_limit_bytes=24 << 20),
        cost_estimate=pl.CostEstimate(
            flops=rows * n_keys * width, bytes_accessed=1 << 20, transcendentals=0
        ),
        name="near",
    )(position, *[in_hbm(x) for x in (queries, keys, values, edge_keys)], edge_values)


def far_kernel(
    tile, heads, members, per_coarse,
    pos_ref, head_ref, q_hbm, m2, m3, m4, mine, other, acc_hbm, peak_hbm, w_hbm,
    att_ref, left_ref, right_ref,
    q_ref, k_ref, v_ref, acc_ref, peak_ref, w_ref, sems, w_sem,
):
    rows, width = att_ref.shape
    n_med, n_coarse = m2.shape[1], mine.shape[0]
    groups = heads // 2

    def whole(src, dst, g, per):
        cols = pl.ds(g * per, per)
        return src.at[:, cols], dst.at[:, cols]

    def part(src, dst, g, to, shift=0):
        size = src.shape[0]
        return (
            src.at[:, pl.ds(shift + g * 2 * HEAD_DIM, 2 * HEAD_DIM)],
            dst.at[pl.ds(to, size), pl.ds(g * 2 * HEAD_DIM, 2 * HEAD_DIM)],
        )

    def group_copies(g):
        pairs = [whole(q_hbm, q_ref, g, 2 * HEAD_DIM)]
        to = 0
        for m in (m2, m3, m4):
            pairs += [part(m.at[0], k_ref, g, to), part(m.at[1], v_ref, g, to)]
            to += n_med
        for c in (mine, other):
            pairs += [part(c, k_ref, g, to), part(c, v_ref, g, to, width)]
            to += n_coarse
        pairs.append(whole(acc_hbm, acc_ref, g, 4 * HEAD_DIM))
        pairs.append(whole(peak_hbm, peak_ref, g, 2 * HEAD_DIM))
        return [
            pltpu.make_async_copy(src, dst, sems.at[t, g]) for t, (src, dst) in enumerate(pairs)
        ]

    copies = [group_copies(g) for g in range(groups)]
    block = lax.rem(head_ref[0] + 2, members)
    cols = pl.ds(pl.multiple_of(block * width, width), width)
    w_copy = pltpu.make_async_copy(w_hbm.at[:, cols], w_ref, w_sem.at[0])
    for g in range(2):
        for copy in copies[g]:
            copy.start()
    w_copy.start()
    pos = pos_ref[0]
    j = lax.broadcasted_iota(jnp.int32, (1, n_coarse), 1) // per_coarse
    group = j // (2 * CHIPS_X)
    step = jnp.where(group == 3, -1, group)
    z = (pos // PLANE + step + 4 * (j % 2)) & (PLANES - 1)
    x = (pos % PLANE // 2 - j // 2 % CHIPS_X) & (CHIPS_X - 1)
    bias = [
        jnp.where(pos >= d, jnp.zeros((1, n_med), F32), jnp.full((1, n_med), NEG, F32))
        for d in (2, 3, 4)
    ]
    for core in (pos % 2, 1 - pos % 2):
        bias.append(jnp.where(z * PLANE + x * 2 + core < pos, 0.0, NEG))
    bias = jnp.concatenate(bias, axis=1)
    for h in range(heads):
        if h % 2 == 0:
            for copy in copies[h // 2]:
                copy.wait()
            if h // 2 + 2 < groups:
                for copy in copies[h // 2 + 2]:
                    copy.start()
        c = head_cols(h)
        for i in range(rows // tile):
            at = pl.ds(i * tile, tile)
            s = mm_t(q_ref[at, c], k_ref[:, c]) + bias
            near_peak = peak_ref[at, c]
            peak = jnp.maximum(near_peak, jnp.max(s, axis=1, keepdims=True))
            shrink = jnp.exp2((near_peak - peak) * EXP2_SCALE)
            got = weigh(s, peak[:, :1], v_ref[:, c])
            near_acc = acc_ref[at, head_cols(2 * h)]
            near_total = acc_ref[at, head_cols(2 * h + 1)]
            att_ref[at, c] = (
                (near_acc * shrink + got[:, :HEAD_DIM])
                / (near_total * shrink + got[:, HEAD_DIM:])
            ).astype(BF16)
    w_copy.wait()
    middle = width // 2
    left_ref[...] = mm(att_ref[...], w_ref[:, :middle]).astype(BF16)
    right_ref[...] = mm(att_ref[...], w_ref[:, middle:]).astype(BF16)


def far(position, head, queries, meds, coarse, acc, peak, weight):
    rows, width = queries.shape
    heads = width // HEAD_DIM
    members = weight.shape[1] // width
    n_keys = 3 * meds[0].shape[1] + 2 * coarse[0].shape[0]
    half = jax.ShapeDtypeStruct((rows, width // 2), BF16)
    return pl.pallas_call(
        functools.partial(far_kernel, 256, heads, members, rows // COARSE),
        out_shape=(jax.ShapeDtypeStruct((rows, width), BF16), half, half),
        in_specs=[SMEM, SMEM] + [HBM] * 9,
        out_specs=(VMEM, VMEM, VMEM),
        scratch_shapes=[
            pltpu.VMEM((rows, width), BF16),
            pltpu.VMEM((n_keys, width), BF16),
            pltpu.VMEM((n_keys, width), BF16),
            pltpu.VMEM((rows, 2 * width), F32),
            pltpu.VMEM((rows, width), F32),
            pltpu.VMEM((width, width), BF16),
            pltpu.SemaphoreType.DMA((13, heads // 2)),
            pltpu.SemaphoreType.DMA((1,)),
        ],
        compiler_params=pltpu.CompilerParams(vmem_limit_bytes=36 << 20),
        cost_estimate=pl.CostEstimate(
            flops=8 * rows * n_keys * width, bytes_accessed=2 << 20, transcendentals=0
        ),
        name="far",
    )(
        position,
        head,
        in_hbm(queries),
        in_hbm(meds[0]),
        meds[1],
        in_hbm(meds[2]),
        *coarse,
        in_hbm(acc),
        in_hbm(peak),
        in_hbm(weight),
    )


def project_kernel(members, order, head_ref, a_ref, w_hbm, *refs):
    outs, (w_ref, sems) = refs[: len(order)], refs[len(order) :]
    width = outs[0].shape[1]
    copies = []
    for i, k in enumerate(order):
        block = lax.rem(head_ref[0] + k, members)
        cols = pl.ds(pl.multiple_of(block * width, width), width)
        copies.append(pltpu.make_async_copy(w_hbm.at[:, cols], w_ref.at[i], sems.at[i]))
        copies[i].start()
    for i, out in enumerate(outs):
        copies[i].wait()
        out[...] = mm(a_ref[...], w_ref[i]).astype(BF16)


def project(head, attention, weight, members, order):
    rows, depth = attention.shape
    width = weight.shape[1] // members
    return pl.pallas_call(
        functools.partial(project_kernel, members, order),
        out_shape=[jax.ShapeDtypeStruct((rows, width), BF16)] * len(order),
        in_specs=[SMEM, VMEM, HBM],
        out_specs=[VMEM] * len(order),
        scratch_shapes=[
            pltpu.VMEM((len(order), depth, width), BF16),
            pltpu.SemaphoreType.DMA((len(order),)),
        ],
        compiler_params=pltpu.CompilerParams(vmem_limit_bytes=24 << 20),
        cost_estimate=pl.CostEstimate(
            flops=2 * rows * depth * width * len(order),
            bytes_accessed=6 << 20,
            transcendentals=0,
        ),
        name="project",
    )(head, attention, in_hbm(weight))


def shifted(block, axis, distance):
    devices = range(lax.axis_size(axis))
    return lax.ppermute(
        block, axis, [(i - distance, i) for i in devices if i - distance in devices]
    )


def body(queries, keys, values, med_weight, coarse_weight, out_weight):
    n_seq = lax.axis_size("seq")
    members = lax.axis_size("head")
    position = lax.axis_index("seq")
    pos = position.astype(jnp.int32).reshape(1)
    head = lax.axis_index("head").astype(jnp.int32).reshape(1)
    core0 = (position & 1) == 0
    swap = [(i, i ^ 1) for i in range(n_seq)]

    def place(z, x, core):
        return z * PLANE + x * 2 + core

    def move(block, dz, dx):
        route = [
            (place(z, x, c), place((z + dz) % PLANES, (x + dx) % CHIPS_X, c))
            for z in range(PLANES)
            for x in range(CHIPS_X)
            for c in range(2)
        ]
        return lax.ppermute(block, "seq", route)

    edge_keys = shifted(keys, "seq", 1)
    med, coarse = pool(keys, values, med_weight, coarse_weight)
    quad = jnp.concatenate([coarse, move(coarse, 4, 0)], 0)
    ring = jnp.concatenate([quad] + [move(quad, 0, d) for d in range(1, CHIPS_X)], 0)

    edge_keys, values, ring, med = lax.optimization_barrier((edge_keys, values, ring, med))
    edge_values = shifted(values, "seq", 1)
    rings = [move(ring, d, 0) for d in (-1, -2, 1)]
    med2 = shifted(med, "seq", 2)
    med4 = shifted(med, "seq", 4)
    acc, peak = near(pos, queries, keys, values, edge_keys, edge_values)
    rings, med2, med4, acc, peak = lax.optimization_barrier((rings, med2, med4, acc, peak))
    mine = jnp.concatenate([ring] + rings, 0)
    other = lax.ppermute(mine, "seq", swap)
    med3 = lax.ppermute(jnp.where(core0, med2, med4), "seq", swap)

    def send(block, distance):
        return lax.ppermute(
            block, "head", [(i, (i + distance) % members) for i in range(members)]
        )

    attention, left, right = far(
        pos, head, queries, (med2, med3, med4), (mine, other), acc, peak, out_weight
    )
    left, right = send(left, 1), send(right, -1)
    ahead, behind, own = project(head, attention, out_weight, members, (1, members - 1, 0))
    middle = left.shape[1]

    def plus(a, b):
        return (a.astype(F32) + b.astype(F32)).astype(BF16)

    ahead = jnp.concatenate([plus(ahead[:, :middle], left), ahead[:, middle:]], 1)
    behind = jnp.concatenate([behind[:, :middle], plus(behind[:, middle:], right)], 1)
    ahead, behind = send(ahead, 1), send(behind, -1)
    return (own.astype(F32) + ahead.astype(F32) + behind.astype(F32)).astype(BF16)


def solution(mesh):
    placed = (
        P("seq", "head"),
        P("seq", "head"),
        P("seq", "head"),
        P(None, "head", None),
        P(None, "head", None),
        P("head", None),
    )
    return jax.shard_map(
        body, mesh=mesh, in_specs=placed, out_specs=P("seq", "head"), check_vma=False
    )
```

```python
import functools
import math

import jax
import jax.numpy as jnp
from jax import lax
from jax.experimental import pallas as pl
from jax.experimental.pallas import tpu as pltpu
from jax.sharding import PartitionSpec as P

HEAD_DIM = 128
WIN = 512
MED = 4
COARSE = 64
CHIPS_X = 4
PLANE = 2 * CHIPS_X
PLANES = 8
NEG = -1e30
EXP2_SCALE = math.log2(math.e) / math.sqrt(HEAD_DIM)
F32 = jnp.float32
BF16 = jnp.bfloat16
HBM = pl.BlockSpec(memory_space=pltpu.HBM)
VMEM = pl.BlockSpec(memory_space=pltpu.VMEM)
SMEM = pl.BlockSpec(memory_space=pltpu.SMEM)


def in_hbm(x):
    return pltpu.with_memory_space_constraint(x, pltpu.HBM)


def mm(a, b):
    return lax.dot_general(a, b, (((1,), (0,)), ((), ())), preferred_element_type=F32)


def mm_t(a, b):
    return lax.dot_general(a, b, (((1,), (1,)), ((), ())), preferred_element_type=F32)


def head_cols(h):
    return pl.ds(h * HEAD_DIM, HEAD_DIM)


def fetch_heads(pairs, sems, heads):
    copies = []
    for h in range(heads):
        copies.append(
            [
                pltpu.make_async_copy(
                    src.at[:, head_cols(h)], dst.at[:, head_cols(h)], sems.at[t, h]
                )
                for t, (src, dst) in enumerate(pairs)
            ]
        )
        for copy in copies[h]:
            copy.start()
    return copies


def pool_kernel(
    heads,
    k_hbm, v_hbm, mw_ref, cw_hbm,
    med_ref, coarse_ref,
    k_ref, v_ref, cw_ref, rows_ref, sems, w_sem,
):
    w_copy = pltpu.make_async_copy(cw_hbm, cw_ref, w_sem.at[0])
    w_copy.start()
    copies = fetch_heads(((k_hbm, k_ref), (v_hbm, v_ref)), sems, heads)
    rows = k_ref.shape[0]
    n_med, n_coarse = rows // MED, rows // COARSE
    lane = lax.broadcasted_iota(jnp.int32, (heads, rows), 1)
    for slot, (ref, ratio) in enumerate(((mw_ref, MED), (cw_ref, COARSE))):
        at = lane % ratio
        if slot:
            w_copy.wait()
        for t in range(2):
            w = ref[t]
            spread = jnp.zeros((heads, rows), F32)
            for r in range(ratio):
                spread = jnp.where(at == r, w[:, r : r + 1], spread)
            high = spread.astype(BF16).astype(F32)
            rows_ref[slot, 0, t] = high
            rows_ref[slot, 1, t] = spread - high

    def on(n, ratio):
        source = lax.broadcasted_iota(jnp.int32, (n, rows), 1)
        return source // ratio == lax.broadcasted_iota(jnp.int32, (n, rows), 0)

    med_on, coarse_on = on(n_med, MED), on(n_coarse, COARSE)
    for h in range(heads):
        for copy in copies[h]:
            copy.wait()
        for t, ref in enumerate((k_ref, v_ref)):
            row = pl.ds(h, 1)
            left = []
            for part in range(2):
                left.append(jnp.where(med_on, rows_ref[0, part, t, row, :], 0.0))
                left.append(jnp.where(coarse_on, rows_ref[1, part, t, row, :], 0.0))
            r = mm(jnp.concatenate(left, axis=0).astype(BF16), ref[:, head_cols(h)])
            r = r[: n_med + n_coarse] + r[n_med + n_coarse :]
            med_ref[t, :, head_cols(h)] = r[:n_med].astype(BF16)
            coarse_ref[:, head_cols(t * heads + h)] = r[n_med:].astype(BF16)


def pool(keys, values, med_weight, coarse_weight):
    rows, width = keys.shape
    heads = width // HEAD_DIM
    return pl.pallas_call(
        functools.partial(pool_kernel, heads),
        out_shape=(jax.ShapeDtypeStruct((2, rows // MED, width), BF16),
            jax.ShapeDtypeStruct((rows // COARSE, 2 * width), BF16),
        ),
        in_specs=[HBM, HBM, VMEM, HBM],
        out_specs=(VMEM, VMEM),
        scratch_shapes=[
            pltpu.VMEM((rows, width), BF16),
            pltpu.VMEM((rows, width), BF16),
            pltpu.VMEM(coarse_weight.shape, F32),
            pltpu.VMEM((2, 2, 2, heads, rows), F32),
            pltpu.SemaphoreType.DMA((2, heads)),
            pltpu.SemaphoreType.DMA((1,)),
        ],
        compiler_params=pltpu.CompilerParams(vmem_limit_bytes=12 << 20),
        cost_estimate=pl.CostEstimate(
            flops=4 * 136 * rows * 2 * width, bytes_accessed=3 << 20, transcendentals=0
        ),
        name="pool",
    )(
        in_hbm(keys),
        in_hbm(values),
        med_weight,
        in_hbm(coarse_weight),
    )


def weigh(scores, peak, values):
    p = jnp.exp2((scores - peak) * EXP2_SCALE).astype(BF16)
    return mm(p, jnp.concatenate([values, jnp.ones_like(values)], axis=1))


def near_kernel(
    tile, heads,
    pos_ref, q_hbm, k_hbm, v_hbm, ek_hbm, ev_hbm,
    acc_hbm, peak_hbm,
    q_ref, k_ref, v_ref, acc_ref, peak_ref, sems, out_sems,
):
    rows, n_edge = q_ref.shape[0], ek_hbm.shape[0]
    own, edge = pl.ds(n_edge, rows), pl.ds(0, n_edge)
    copies = fetch_heads(
        (
            (q_hbm, q_ref),
            (k_hbm, k_ref.at[own, :]),
            (v_hbm, v_ref.at[own, :]),
            (ek_hbm, k_ref.at[edge, :]),
            (ev_hbm, v_ref.at[edge, :]),
        ),
        sems,
        heads,
    )
    has_edge = pos_ref[0] >= 1
    written = []
    on_diag = lax.broadcasted_iota(jnp.int32, (tile, tile), 1) <= lax.broadcasted_iota(
        jnp.int32, (tile, tile), 0
    )
    for h in range(heads):
        for copy in copies[h]:
            copy.wait()
        c = head_cols(h)
        for i in range(rows // tile):
            at, n = pl.ds(i * tile, tile), n_edge + i * tile
            s = mm_t(q_ref[at, c], k_ref[: n + tile, c])
            parts = [jnp.where(has_edge, s[:, :n_edge], NEG)]
            if i:
                parts.append(s[:, n_edge:n])
            parts.append(jnp.where(on_diag, s[:, n:], NEG))
            s = jnp.concatenate(parts, axis=1)
            peak = jnp.max(s, axis=1, keepdims=True)
            acc_ref[at, pl.ds(2 * h * HEAD_DIM, 2 * HEAD_DIM)] = weigh(
                s, peak, v_ref[: n + tile, c]
            )
            peak_ref[at, c] = jnp.broadcast_to(peak, (tile, HEAD_DIM))
        c2 = pl.ds(2 * h * HEAD_DIM, 2 * HEAD_DIM)
        written.append(
            [
                pltpu.make_async_copy(acc_ref.at[:, c2], acc_hbm.at[:, c2], out_sems.at[0, h]),
                pltpu.make_async_copy(peak_ref.at[:, c], peak_hbm.at[:, c], out_sems.at[1, h]),
            ]
        )
        for copy in written[h]:
            copy.start()
    for pair in written:
        for copy in pair:
            copy.wait()


def near(position, queries, keys, values, edge_keys, edge_values):
    rows, width = queries.shape
    heads = width // HEAD_DIM
    n_keys = edge_keys.shape[0] + rows
    return pl.pallas_call(
        functools.partial(near_kernel, 256, heads),
        out_shape=(pltpu.HBM((rows, 2 * width), F32), pltpu.HBM((rows, width), F32)),
        in_specs=[SMEM] + [HBM] * 5,
        out_specs=(HBM, HBM),
        scratch_shapes=[
            pltpu.VMEM((rows, width), BF16),
            pltpu.VMEM((n_keys, width), BF16),
            pltpu.VMEM((n_keys, width), BF16),
            pltpu.VMEM((rows, 2 * width), F32),
            pltpu.VMEM((rows, width), F32),
            pltpu.SemaphoreType.DMA((5, heads)),
            pltpu.SemaphoreType.DMA((2, heads)),
        ],
        compiler_params=pltpu.CompilerParams(vmem_limit_bytes=32 << 20),
        cost_estimate=pl.CostEstimate(
            flops=rows * n_keys * width, bytes_accessed=1 << 20, transcendentals=0
        ),
        name="near",
    )(position, *[in_hbm(x) for x in (queries, keys, values, edge_keys)], edge_values)


def far_kernel(
    tile, heads, members, per_coarse,
    pos_ref, head_ref, q_hbm, m2, m3_even, m3_odd, m4, mine, other, acc_hbm, peak_hbm, w_hbm,
    att_ref, left_ref, right_ref,
    q_ref, k_ref, v_ref, acc_ref, peak_ref, w_ref, sems, w_sem,
):
    rows, width = att_ref.shape
    n_med, n_coarse = m2.shape[1], mine.shape[0]
    groups = heads // 2

    def whole(src, dst, g, per):
        cols = pl.ds(g * per, per)
        return src.at[:, cols], dst.at[:, cols]

    def part(src, dst, g, to, shift=0):
        size = src.shape[0]
        return (
            src.at[:, pl.ds(shift + g * 2 * HEAD_DIM, 2 * HEAD_DIM)],
            dst.at[pl.ds(to, size), pl.ds(g * 2 * HEAD_DIM, 2 * HEAD_DIM)],
        )

    def group_copies(g, m3):
        pairs = [whole(q_hbm, q_ref, g, 2 * HEAD_DIM)]
        to = 0
        for m in (m3, m2, m4):
            pairs += [part(m.at[0], k_ref, g, to), part(m.at[1], v_ref, g, to)]
            to += n_med
        for c in (mine, other):
            pairs += [part(c, k_ref, g, to), part(c, v_ref, g, to, width)]
            to += n_coarse
        pairs.append(whole(acc_hbm, acc_ref, g, 4 * HEAD_DIM))
        pairs.append(whole(peak_hbm, peak_ref, g, 2 * HEAD_DIM))
        return [
            pltpu.make_async_copy(src, dst, sems.at[t, g]) for t, (src, dst) in enumerate(pairs)
        ]

    copies = [group_copies(g, m3_even) for g in range(groups)]
    even = pos_ref[0] % 2 == 0

    def start(g):
        @pl.when(even)
        def _():
            for copy in copies[g][1:3]:
                copy.start()

        @pl.when(jnp.logical_not(even))
        def _():
            for copy in group_copies(g, m3_odd)[1:3]:
                copy.start()

        for copy in copies[g][:1] + copies[g][3:]:
            copy.start()

    block = lax.rem(head_ref[0] + 2, members)
    cols = pl.ds(pl.multiple_of(block * width, width), width)
    w_copy = pltpu.make_async_copy(w_hbm.at[:, cols], w_ref, w_sem.at[0])
    for g in range(2):
        start(g)
    w_copy.start()
    pos = pos_ref[0]
    j = lax.broadcasted_iota(jnp.int32, (1, n_coarse), 1) // per_coarse
    group = j // (2 * CHIPS_X)
    step = jnp.where(group == 3, -1, group)
    z = (pos // PLANE + step + 4 * (j % 2)) & (PLANES - 1)
    x = (pos % PLANE // 2 - j // 2 % CHIPS_X) & (CHIPS_X - 1)
    bias = [
        jnp.where(pos >= d, jnp.zeros((1, n_med), F32), jnp.full((1, n_med), NEG, F32))
        for d in (3, 2, 4)
    ]
    for core in (pos % 2, 1 - pos % 2):
        bias.append(jnp.where(z * PLANE + x * 2 + core < pos, 0.0, NEG))
    bias = jnp.concatenate(bias, axis=1)
    for h in range(heads):
        if h % 2 == 0:
            for copy in copies[h // 2]:
                copy.wait()
            if h // 2 + 2 < groups:
                start(h // 2 + 2)
        c = head_cols(h)
        for i in range(rows // tile):
            at = pl.ds(i * tile, tile)
            s = mm_t(q_ref[at, c], k_ref[:, c]) + bias
            near_peak = peak_ref[at, c]
            peak = jnp.maximum(near_peak, jnp.max(s, axis=1, keepdims=True))
            shrink = jnp.exp2((near_peak - peak) * EXP2_SCALE)
            got = weigh(s, peak[:, :1], v_ref[:, c])
            near_acc = acc_ref[at, head_cols(2 * h)]
            near_total = acc_ref[at, head_cols(2 * h + 1)]
            att_ref[at, c] = (
                (near_acc * shrink + got[:, :HEAD_DIM])
                / (near_total * shrink + got[:, HEAD_DIM:])
            ).astype(BF16)
    w_copy.wait()
    middle = width // 2
    left_ref[...] = mm(att_ref[...], w_ref[:, :middle]).astype(BF16)
    right_ref[...] = mm(att_ref[...], w_ref[:, middle:]).astype(BF16)


def far(position, head, queries, meds, coarse, acc, peak, weight):
    rows, width = queries.shape
    heads = width // HEAD_DIM
    members = weight.shape[1] // width
    n_keys = 3 * meds[0].shape[1] + 2 * coarse[0].shape[0]
    half = jax.ShapeDtypeStruct((rows, width // 2), BF16)
    return pl.pallas_call(
        functools.partial(far_kernel, 256, heads, members, rows // COARSE),
        out_shape=(jax.ShapeDtypeStruct((rows, width), BF16), half, half),
        in_specs=[SMEM, SMEM] + [HBM] * 10,
        out_specs=(VMEM, VMEM, VMEM),
        scratch_shapes=[
            pltpu.VMEM((rows, width), BF16),
            pltpu.VMEM((n_keys, width), BF16),
            pltpu.VMEM((n_keys, width), BF16),
            pltpu.VMEM((rows, 2 * width), F32),
            pltpu.VMEM((rows, width), F32),
            pltpu.VMEM((width, width), BF16),
            pltpu.SemaphoreType.DMA((13, heads // 2)),
            pltpu.SemaphoreType.DMA((1,)),
        ],
        compiler_params=pltpu.CompilerParams(vmem_limit_bytes=36 << 20),
        cost_estimate=pl.CostEstimate(
            flops=8 * rows * n_keys * width, bytes_accessed=2 << 20, transcendentals=0
        ),
        name="far",
    )(
        position,
        head,
        in_hbm(queries),
        in_hbm(meds[0]),
        *meds[1:3],
        in_hbm(meds[3]),
        *coarse,
        in_hbm(acc),
        in_hbm(peak),
        in_hbm(weight),
    )


def project_kernel(members, order, head_ref, a_ref, w_hbm, *refs):
    outs, (w_ref, sems) = refs[: len(order)], refs[len(order) :]
    width = outs[0].shape[1]
    copies = []
    for i, k in enumerate(order):
        block = lax.rem(head_ref[0] + k, members)
        cols = pl.ds(pl.multiple_of(block * width, width), width)
        copies.append(pltpu.make_async_copy(w_hbm.at[:, cols], w_ref.at[i], sems.at[i]))
        copies[i].start()
    for i, out in enumerate(outs):
        copies[i].wait()
        out[...] = mm(a_ref[...], w_ref[i]).astype(BF16)


def project(head, attention, weight, members, order):
    rows, depth = attention.shape
    width = weight.shape[1] // members
    return pl.pallas_call(
        functools.partial(project_kernel, members, order),
        out_shape=[jax.ShapeDtypeStruct((rows, width), BF16)] * len(order),
        in_specs=[SMEM, VMEM, HBM],
        out_specs=[VMEM] * len(order),
        scratch_shapes=[
            pltpu.VMEM((len(order), depth, width), BF16),
            pltpu.SemaphoreType.DMA((len(order),)),
        ],
        compiler_params=pltpu.CompilerParams(vmem_limit_bytes=24 << 20),
        cost_estimate=pl.CostEstimate(
            flops=2 * rows * depth * width * len(order),
            bytes_accessed=6 << 20,
            transcendentals=0,
        ),
        name="project",
    )(head, attention, in_hbm(weight))


def shifted(block, axis, distance):
    devices = range(lax.axis_size(axis))
    return lax.ppermute(
        block, axis, [(i - distance, i) for i in devices if i - distance in devices]
    )


def body(queries, keys, values, med_weight, coarse_weight, out_weight):
    n_seq = lax.axis_size("seq")
    members = lax.axis_size("head")
    position = lax.axis_index("seq")
    pos = position.astype(jnp.int32).reshape(1)
    head = lax.axis_index("head").astype(jnp.int32).reshape(1)
    swap = [(i, i ^ 1) for i in range(n_seq)]

    def place(z, x, core):
        return z * PLANE + x * 2 + core

    def move(block, dz, dx):
        route = [
            (place(z, x, c), place((z + dz) % PLANES, (x + dx) % CHIPS_X, c))
            for z in range(PLANES)
            for x in range(CHIPS_X)
            for c in range(2)
        ]
        return lax.ppermute(block, "seq", route)

    edge_keys = shifted(keys, "seq", 1)
    med, coarse = pool(keys, values, med_weight, coarse_weight)
    quad = jnp.concatenate([coarse, move(coarse, 4, 0)], 0)
    ring = jnp.concatenate([quad] + [move(quad, 0, d) for d in range(1, CHIPS_X)], 0)

    edge_keys, values, ring, med = lax.optimization_barrier((edge_keys, values, ring, med))
    edge_values = shifted(values, "seq", 1)
    rings = [move(ring, d, 0) for d in (-1, -2, 1)]
    turned = move(med, 0, -1)
    rings, edge_values, turned, med = lax.optimization_barrier((rings, edge_values, turned, med))
    med2 = shifted(med, "seq", 2)
    last = [
        (place(z, x, c), place(z + (x + 1) % CHIPS_X // 2, (x - 1) % CHIPS_X, c))
        for z in range(PLANES)
        for x in range(CHIPS_X)
        for c in range(2)
        if z + (x + 1) % CHIPS_X // 2 < PLANES
    ]
    med4 = lax.ppermute(turned, "seq", last)
    acc, peak = near(pos, queries, keys, values, edge_keys, edge_values)
    med2, med4, acc, peak = lax.optimization_barrier((med2, med4, acc, peak))
    mine = jnp.concatenate([ring] + rings, 0)
    other = lax.ppermute(mine, "seq", swap)
    med3_even = lax.ppermute(med4, "seq", [(i + 1, i) for i in range(0, n_seq, 2)])
    med3_odd = lax.ppermute(med2, "seq", [(i, i + 1) for i in range(0, n_seq, 2)])

    def send(block, distance):
        return lax.ppermute(
            block, "head", [(i, (i + distance) % members) for i in range(members)]
        )

    attention, left, right = far(
        pos, head, queries, (med2, med3_even, med3_odd, med4), (mine, other), acc, peak, out_weight
    )
    left, right = send(left, 1), send(right, -1)
    ahead, behind, own = project(head, attention, out_weight, members, (1, members - 1, 0))
    middle = left.shape[1]

    def plus(a, b):
        return (a.astype(F32) + b.astype(F32)).astype(BF16)

    ahead = jnp.concatenate([plus(ahead[:, :middle], left), ahead[:, middle:]], 1)
    behind = jnp.concatenate([behind[:, :middle], plus(behind[:, middle:], right)], 1)
    ahead, behind = send(ahead, 1), send(behind, -1)
    return (own.astype(F32) + ahead.astype(F32) + behind.astype(F32)).astype(BF16)


def solution(mesh):
    placed = (
        P("seq", "head"),
        P("seq", "head"),
        P("seq", "head"),
        P(None, "head", None),
        P(None, "head", None),
        P("head", None),
    )
    return jax.shard_map(
        body, mesh=mesh, in_specs=placed, out_specs=P("seq", "head"), check_vma=False
    )
```

```python
import functools
import math

import jax
import jax.numpy as jnp
from jax import lax
from jax.experimental import pallas as pl
from jax.experimental.pallas import tpu as pltpu
from jax.sharding import PartitionSpec as P

HEAD_DIM = 128
WIN = 512
MED = 4
COARSE = 64
CHIPS_X = 4
PLANE = 2 * CHIPS_X
PLANES = 8
CHUNKS = 2
NEG = -1e30
EXP2_SCALE = math.log2(math.e) / math.sqrt(HEAD_DIM)
F32 = jnp.float32
BF16 = jnp.bfloat16
HBM = pl.BlockSpec(memory_space=pltpu.HBM)
VMEM = pl.BlockSpec(memory_space=pltpu.VMEM)
SMEM = pl.BlockSpec(memory_space=pltpu.SMEM)


def in_hbm(x):
    return pltpu.with_memory_space_constraint(x, pltpu.HBM)


def mm(a, b):
    return lax.dot_general(a, b, (((1,), (0,)), ((), ())), preferred_element_type=F32)


def mm_t(a, b):
    return lax.dot_general(a, b, (((1,), (1,)), ((), ())), preferred_element_type=F32)


def head_cols(h):
    return pl.ds(h * HEAD_DIM, HEAD_DIM)


def fetch_heads(pairs, sems, heads):
    copies = []
    for h in range(heads):
        copies.append(
            [
                pltpu.make_async_copy(
                    src.at[:, head_cols(h)], dst.at[:, head_cols(h)], sems.at[t, h]
                )
                for t, (src, dst) in enumerate(pairs)
            ]
        )
        for copy in copies[h]:
            copy.start()
    return copies


def pool_kernel(
    heads,
    k_hbm, v_hbm, mw_ref, cw_hbm,
    med_ref, coarse_ref,
    k_ref, v_ref, cw_ref, rows_ref, sems, w_sem,
):
    w_copy = pltpu.make_async_copy(cw_hbm, cw_ref, w_sem.at[0])
    w_copy.start()
    copies = fetch_heads(((k_hbm, k_ref), (v_hbm, v_ref)), sems, heads)
    rows = k_ref.shape[0]
    n_med, n_coarse = rows // MED, rows // COARSE
    lane = lax.broadcasted_iota(jnp.int32, (heads, rows), 1)
    for slot, (ref, ratio) in enumerate(((mw_ref, MED), (cw_ref, COARSE))):
        at = lane % ratio
        if slot:
            w_copy.wait()
        for t in range(2):
            w = ref[t]
            spread = jnp.zeros((heads, rows), F32)
            for r in range(ratio):
                spread = jnp.where(at == r, w[:, r : r + 1], spread)
            high = spread.astype(BF16).astype(F32)
            rows_ref[slot, 0, t] = high
            rows_ref[slot, 1, t] = spread - high

    def on(n, ratio):
        source = lax.broadcasted_iota(jnp.int32, (n, rows), 1)
        return source // ratio == lax.broadcasted_iota(jnp.int32, (n, rows), 0)

    med_on, coarse_on = on(n_med, MED), on(n_coarse, COARSE)
    for h in range(heads):
        for copy in copies[h]:
            copy.wait()
        for t, ref in enumerate((k_ref, v_ref)):
            row = pl.ds(h, 1)
            left = []
            for part in range(2):
                left.append(jnp.where(med_on, rows_ref[0, part, t, row, :], 0.0))
                left.append(jnp.where(coarse_on, rows_ref[1, part, t, row, :], 0.0))
            r = mm(jnp.concatenate(left, axis=0).astype(BF16), ref[:, head_cols(h)])
            r = r[: n_med + n_coarse] + r[n_med + n_coarse :]
            med_ref[t, :, head_cols(h)] = r[:n_med].astype(BF16)
            coarse_ref[:, head_cols(t * heads + h)] = r[n_med:].astype(BF16)


def pool(keys, values, med_weight, coarse_weight):
    rows, width = keys.shape
    heads = width // HEAD_DIM
    return pl.pallas_call(
        functools.partial(pool_kernel, heads),
        out_shape=(jax.ShapeDtypeStruct((2, rows // MED, width), BF16),
            jax.ShapeDtypeStruct((rows // COARSE, 2 * width), BF16),
        ),
        in_specs=[HBM, HBM, VMEM, HBM],
        out_specs=(VMEM, VMEM),
        scratch_shapes=[
            pltpu.VMEM((rows, width), BF16),
            pltpu.VMEM((rows, width), BF16),
            pltpu.VMEM(coarse_weight.shape, F32),
            pltpu.VMEM((2, 2, 2, heads, rows), F32),
            pltpu.SemaphoreType.DMA((2, heads)),
            pltpu.SemaphoreType.DMA((1,)),
        ],
        compiler_params=pltpu.CompilerParams(vmem_limit_bytes=12 << 20),
        cost_estimate=pl.CostEstimate(
            flops=4 * 136 * rows * 2 * width, bytes_accessed=3 << 20, transcendentals=0
        ),
        name="pool",
    )(
        in_hbm(keys),
        in_hbm(values),
        med_weight,
        in_hbm(coarse_weight),
    )


def weigh(scores, peak, values):
    p = jnp.exp2((scores - peak) * EXP2_SCALE).astype(BF16)
    return mm(p, jnp.concatenate([values, jnp.ones_like(values)], axis=1))


def near_kernel(
    tile, heads,
    pos_ref, q_hbm, k_hbm, v_hbm, ek_hbm, ev_hbm,
    acc_hbm, peak_hbm,
    q_ref, k_ref, v_ref, acc_ref, peak_ref, sems, out_sems,
):
    rows, n_edge = q_ref.shape[0], ek_hbm.shape[0]
    own, edge = pl.ds(n_edge, rows), pl.ds(0, n_edge)
    copies = fetch_heads(
        (
            (q_hbm, q_ref),
            (k_hbm, k_ref.at[own, :]),
            (v_hbm, v_ref.at[own, :]),
            (ek_hbm, k_ref.at[edge, :]),
            (ev_hbm, v_ref.at[edge, :]),
        ),
        sems,
        heads,
    )
    has_edge = pos_ref[0] >= 1
    written = []
    on_diag = lax.broadcasted_iota(jnp.int32, (tile, tile), 1) <= lax.broadcasted_iota(
        jnp.int32, (tile, tile), 0
    )
    for h in range(heads):
        for copy in copies[h]:
            copy.wait()
        c = head_cols(h)
        for i in range(rows // tile):
            at, n = pl.ds(i * tile, tile), n_edge + i * tile
            s = mm_t(q_ref[at, c], k_ref[: n + tile, c])
            parts = [jnp.where(has_edge, s[:, :n_edge], NEG)]
            if i:
                parts.append(s[:, n_edge:n])
            parts.append(jnp.where(on_diag, s[:, n:], NEG))
            s = jnp.concatenate(parts, axis=1)
            peak = jnp.max(s, axis=1, keepdims=True)
            acc_ref[at, pl.ds(2 * h * HEAD_DIM, 2 * HEAD_DIM)] = weigh(
                s, peak, v_ref[: n + tile, c]
            )
            peak_ref[at, c] = jnp.broadcast_to(peak, (tile, HEAD_DIM))
        c2 = pl.ds(2 * h * HEAD_DIM, 2 * HEAD_DIM)
        written.append(
            [
                pltpu.make_async_copy(acc_ref.at[:, c2], acc_hbm.at[:, c2], out_sems.at[0, h]),
                pltpu.make_async_copy(peak_ref.at[:, c], peak_hbm.at[:, c], out_sems.at[1, h]),
            ]
        )
        for copy in written[h]:
            copy.start()
    for pair in written:
        for copy in pair:
            copy.wait()


def near(position, queries, keys, values, edge_keys, edge_values):
    rows, width = queries.shape
    heads = width // HEAD_DIM
    n_keys = edge_keys.shape[0] + rows
    return pl.pallas_call(
        functools.partial(near_kernel, 256, heads),
        out_shape=(pltpu.HBM((rows, 2 * width), F32), pltpu.HBM((rows, width), F32)),
        in_specs=[SMEM] + [HBM] * 5,
        out_specs=(HBM, HBM),
        scratch_shapes=[
            pltpu.VMEM((rows, width), BF16),
            pltpu.VMEM((n_keys, width), BF16),
            pltpu.VMEM((n_keys, width), BF16),
            pltpu.VMEM((rows, 2 * width), F32),
            pltpu.VMEM((rows, width), F32),
            pltpu.SemaphoreType.DMA((5, heads)),
            pltpu.SemaphoreType.DMA((2, heads)),
        ],
        compiler_params=pltpu.CompilerParams(vmem_limit_bytes=32 << 20),
        cost_estimate=pl.CostEstimate(
            flops=rows * n_keys * width, bytes_accessed=1 << 20, transcendentals=0
        ),
        name="near",
    )(position, *[in_hbm(x) for x in (queries, keys, values, edge_keys)], edge_values)


def far_kernel(
    first_row, heads, members, per_coarse,
    pos_ref, head_ref, q_hbm, m2, m3, m4, mine, other, acc_hbm, peak_hbm, w_hbm,
    att_ref, left_ref, right_ref,
    q_ref, k_ref, v_ref, acc_ref, peak_ref, w_ref, sems, w_sem,
):
    rows, width = att_ref.shape
    n_med, n_coarse = m2.shape[1], mine.shape[0]
    groups = heads // 2

    def whole(src, dst, g, per):
        cols = pl.ds(g * per, per)
        return src.at[pl.ds(first_row, rows), cols], dst.at[:, cols]

    def part(src, dst, g, to, shift=0):
        size = src.shape[0]
        return (
            src.at[:, pl.ds(shift + g * 2 * HEAD_DIM, 2 * HEAD_DIM)],
            dst.at[pl.ds(to, size), pl.ds(g * 2 * HEAD_DIM, 2 * HEAD_DIM)],
        )

    def group_copies(g):
        pairs = [whole(q_hbm, q_ref, g, 2 * HEAD_DIM)]
        to = 0
        for m in (m2, m3, m4):
            pairs += [part(m.at[0], k_ref, g, to), part(m.at[1], v_ref, g, to)]
            to += n_med
        for c in (mine, other):
            pairs += [part(c, k_ref, g, to), part(c, v_ref, g, to, width)]
            to += n_coarse
        pairs.append(whole(acc_hbm, acc_ref, g, 4 * HEAD_DIM))
        pairs.append(whole(peak_hbm, peak_ref, g, 2 * HEAD_DIM))
        return [
            pltpu.make_async_copy(src, dst, sems.at[t, g]) for t, (src, dst) in enumerate(pairs)
        ]

    copies = [group_copies(g) for g in range(groups)]

    def start(g):
        for copy in copies[g]:
            copy.start()

    block = lax.rem(head_ref[0] + 2, members)
    cols = pl.ds(pl.multiple_of(block * width, width), width)
    w_copy = pltpu.make_async_copy(w_hbm.at[:, cols], w_ref, w_sem.at[0])
    for g in range(2):
        start(g)
    w_copy.start()
    pos = pos_ref[0]
    j = lax.broadcasted_iota(jnp.int32, (1, n_coarse), 1) // per_coarse
    group = j // (2 * CHIPS_X)
    step = jnp.where(group == 3, -1, group)
    z = (pos // PLANE + step + 4 * (j % 2)) & (PLANES - 1)
    x = (pos % PLANE // 2 - j // 2 % CHIPS_X) & (CHIPS_X - 1)
    bias = [
        jnp.where(pos >= d, jnp.zeros((1, n_med), F32), jnp.full((1, n_med), NEG, F32))
        for d in (2, 3, 4)
    ]
    for core in (pos % 2, 1 - pos % 2):
        bias.append(jnp.where(z * PLANE + x * 2 + core < pos, 0.0, NEG))
    bias = jnp.concatenate(bias, axis=1)
    for h in range(heads):
        if h % 2 == 0:
            for copy in copies[h // 2]:
                copy.wait()
            if h // 2 + 2 < groups:
                start(h // 2 + 2)
        c = head_cols(h)
        s = mm_t(q_ref[:, c], k_ref[:, c]) + bias
        near_peak = peak_ref[:, c]
        peak = jnp.maximum(near_peak, jnp.max(s, axis=1, keepdims=True))
        shrink = jnp.exp2((near_peak - peak) * EXP2_SCALE)
        got = weigh(s, peak[:, :1], v_ref[:, c])
        near_acc = acc_ref[:, head_cols(2 * h)]
        near_total = acc_ref[:, head_cols(2 * h + 1)]
        att_ref[:, c] = (
            (near_acc * shrink + got[:, :HEAD_DIM]) / (near_total * shrink + got[:, HEAD_DIM:])
        ).astype(BF16)
    w_copy.wait()
    middle = width // 2
    left_ref[...] = mm(att_ref[...], w_ref[:, :middle]).astype(BF16)
    right_ref[...] = mm(att_ref[...], w_ref[:, middle:]).astype(BF16)


def far(position, head, queries, meds, coarse, acc, peak, weight, first_row, rows):
    block, width = queries.shape
    heads = width // HEAD_DIM
    members = weight.shape[1] // width
    n_keys = 3 * meds[0].shape[1] + 2 * coarse[0].shape[0]
    half = jax.ShapeDtypeStruct((rows, width // 2), BF16)
    return pl.pallas_call(
        functools.partial(far_kernel, first_row, heads, members, block // COARSE),
        out_shape=(jax.ShapeDtypeStruct((rows, width), BF16), half, half),
        in_specs=[SMEM, SMEM] + [HBM] * 9,
        out_specs=(VMEM, VMEM, VMEM),
        scratch_shapes=[
            pltpu.VMEM((rows, width), BF16),
            pltpu.VMEM((n_keys, width), BF16),
            pltpu.VMEM((n_keys, width), BF16),
            pltpu.VMEM((rows, 2 * width), F32),
            pltpu.VMEM((rows, width), F32),
            pltpu.VMEM((width, width), BF16),
            pltpu.SemaphoreType.DMA((13, heads // 2)),
            pltpu.SemaphoreType.DMA((1,)),
        ],
        compiler_params=pltpu.CompilerParams(vmem_limit_bytes=36 << 20),
        cost_estimate=pl.CostEstimate(
            flops=8 * rows * n_keys * width, bytes_accessed=2 << 20, transcendentals=0
        ),
        name="far",
    )(
        position,
        head,
        in_hbm(queries),
        in_hbm(meds[0]),
        meds[1],
        in_hbm(meds[2]),
        *coarse,
        in_hbm(acc),
        in_hbm(peak),
        in_hbm(weight),
    )


def project_kernel(members, order, head_ref, a_ref, w_hbm, *refs):
    outs, (w_ref, sems) = refs[: len(order)], refs[len(order) :]
    width = outs[0].shape[1]
    copies = []
    for i, k in enumerate(order):
        block = lax.rem(head_ref[0] + k, members)
        cols = pl.ds(pl.multiple_of(block * width, width), width)
        copies.append(pltpu.make_async_copy(w_hbm.at[:, cols], w_ref.at[i], sems.at[i]))
        copies[i].start()
    for i, out in enumerate(outs):
        copies[i].wait()
        out[...] = mm(a_ref[...], w_ref[i]).astype(BF16)


def project(head, attention, weight, members, order):
    rows, depth = attention.shape
    width = weight.shape[1] // members
    return pl.pallas_call(
        functools.partial(project_kernel, members, order),
        out_shape=[jax.ShapeDtypeStruct((rows, width), BF16)] * len(order),
        in_specs=[SMEM, VMEM, HBM],
        out_specs=[VMEM] * len(order),
        scratch_shapes=[
            pltpu.VMEM((len(order), depth, width), BF16),
            pltpu.SemaphoreType.DMA((len(order),)),
        ],
        compiler_params=pltpu.CompilerParams(vmem_limit_bytes=24 << 20),
        cost_estimate=pl.CostEstimate(
            flops=2 * rows * depth * width * len(order),
            bytes_accessed=6 << 20,
            transcendentals=0,
        ),
        name="project",
    )(head, attention, in_hbm(weight))


def shifted(block, axis, distance):
    devices = range(lax.axis_size(axis))
    return lax.ppermute(
        block, axis, [(i - distance, i) for i in devices if i - distance in devices]
    )


def body(queries, keys, values, med_weight, coarse_weight, out_weight):
    n_seq = lax.axis_size("seq")
    members = lax.axis_size("head")
    position = lax.axis_index("seq")
    pos = position.astype(jnp.int32).reshape(1)
    head = lax.axis_index("head").astype(jnp.int32).reshape(1)
    swap = [(i, i ^ 1) for i in range(n_seq)]

    def place(z, x, core):
        return z * PLANE + x * 2 + core

    def move(block, dz, dx):
        route = [
            (place(z, x, c), place((z + dz) % PLANES, (x + dx) % CHIPS_X, c))
            for z in range(PLANES)
            for x in range(CHIPS_X)
            for c in range(2)
        ]
        return lax.ppermute(block, "seq", route)

    edge_keys = shifted(keys, "seq", 1)
    med, coarse = pool(keys, values, med_weight, coarse_weight)
    quad = jnp.concatenate([coarse, move(coarse, 4, 0)], 0)
    ring = jnp.concatenate([quad] + [move(quad, 0, d) for d in range(1, CHIPS_X)], 0)

    edge_keys, values, ring, med = lax.optimization_barrier((edge_keys, values, ring, med))
    edge_values = shifted(values, "seq", 1)
    below = move(ring, -1, 0)
    turned = move(med, 0, -1)
    below, edge_values, turned, med, ring = lax.optimization_barrier(
        (below, edge_values, turned, med, ring)
    )
    med2 = shifted(med, "seq", 2)
    last = [
        (place(z, x, c), place(z + (x + 1) % CHIPS_X // 2, (x - 1) % CHIPS_X, c))
        for z in range(PLANES)
        for x in range(CHIPS_X)
        for c in range(2)
        if z + (x + 1) % CHIPS_X // 2 < PLANES
    ]
    med4 = lax.ppermute(turned, "seq", last)
    rings = [move(ring, d, 0) for d in (-2, 1)]
    acc, peak = near(pos, queries, keys, values, edge_keys, edge_values)
    rings, med2, med4, acc, peak = lax.optimization_barrier((rings, med2, med4, acc, peak))
    mine = jnp.concatenate([ring, below] + rings, 0)
    other = lax.ppermute(mine, "seq", swap)
    med3 = lax.ppermute(jnp.where(pos % 2 == 0, med2, med4), "seq", swap)

    def send(block, distance):
        return lax.ppermute(
            block, "head", [(i, (i + distance) % members) for i in range(members)]
        )

    def plus(*blocks):
        return functools.reduce(jnp.add, [x.astype(F32) for x in blocks]).astype(BF16)

    rows = queries.shape[0] // CHUNKS
    parts = []
    for c in range(CHUNKS):
        attention, left, right = far(
            pos,
            head,
            queries,
            (med2, med3, med4),
            (mine, other),
            acc,
            peak,
            out_weight,
            c * rows,
            rows,
        )
        attention, pos = lax.optimization_barrier((attention, pos))
        if parts:
            parts[-1], (attention, left, right) = lax.optimization_barrier(
                (parts[-1], (attention, left, right))
            )
        parts.append((attention, send(left, 1), send(right, -1)))
    pieces = []
    for attention, left, right in parts:
        ahead, behind, own = project(head, attention, out_weight, members, (1, members - 1, 0))
        middle = left.shape[1]
        ahead = jnp.concatenate([plus(ahead[:, :middle], left), ahead[:, middle:]], 1)
        behind = jnp.concatenate([behind[:, :middle], plus(behind[:, middle:], right)], 1)
        pieces.append(plus(own, send(ahead, 1), send(behind, -1)))
    return jnp.concatenate(pieces, axis=0)


def solution(mesh):
    placed = (
        P("seq", "head"),
        P("seq", "head"),
        P("seq", "head"),
        P(None, "head", None),
        P(None, "head", None),
        P("head", None),
    )
    return jax.shard_map(
        body, mesh=mesh, in_specs=placed, out_specs=P("seq", "head"), check_vma=False
    )
```

```python
import functools
import math

import jax
import jax.numpy as jnp
from jax import lax
from jax.experimental import pallas as pl
from jax.experimental.pallas import tpu as pltpu
from jax.sharding import PartitionSpec as P

HEAD_DIM = 128
WIN = 512
MED = 4
COARSE = 64
CHIPS_X = 4
PLANE = 2 * CHIPS_X
PLANES = 8
CHUNKS = 2
NEG = -1e30
EXP2_SCALE = math.log2(math.e) / math.sqrt(HEAD_DIM)
F32 = jnp.float32
BF16 = jnp.bfloat16
HBM = pl.BlockSpec(memory_space=pltpu.HBM)
VMEM = pl.BlockSpec(memory_space=pltpu.VMEM)
SMEM = pl.BlockSpec(memory_space=pltpu.SMEM)


def in_hbm(x):
    return pltpu.with_memory_space_constraint(x, pltpu.HBM)


def mm(a, b):
    return lax.dot_general(a, b, (((1,), (0,)), ((), ())), preferred_element_type=F32)


def mm_t(a, b):
    return lax.dot_general(a, b, (((1,), (1,)), ((), ())), preferred_element_type=F32)


def head_cols(h):
    return pl.ds(h * HEAD_DIM, HEAD_DIM)


def fetch_heads(pairs, sems, heads):
    copies = []
    for h in range(heads):
        copies.append(
            [
                pltpu.make_async_copy(
                    src.at[:, head_cols(h)], dst.at[:, head_cols(h)], sems.at[t, h]
                )
                for t, (src, dst) in enumerate(pairs)
            ]
        )
        for copy in copies[h]:
            copy.start()
    return copies


def pool_kernel(
    heads,
    k_hbm, v_hbm, mw_ref, cw_hbm,
    med_ref, coarse_ref,
    k_ref, v_ref, cw_ref, rows_ref, sems, w_sem,
):
    w_copy = pltpu.make_async_copy(cw_hbm, cw_ref, w_sem.at[0])
    w_copy.start()
    copies = fetch_heads(((k_hbm, k_ref), (v_hbm, v_ref)), sems, heads)
    rows = k_ref.shape[0]
    n_med, n_coarse = rows // MED, rows // COARSE
    lane = lax.broadcasted_iota(jnp.int32, (heads, rows), 1)
    for slot, (ref, ratio) in enumerate(((mw_ref, MED), (cw_ref, COARSE))):
        at = lane % ratio
        if slot:
            w_copy.wait()
        for t in range(2):
            w = ref[t]
            spread = jnp.zeros((heads, rows), F32)
            for r in range(ratio):
                spread = jnp.where(at == r, w[:, r : r + 1], spread)
            high = spread.astype(BF16).astype(F32)
            rows_ref[slot, 0, t] = high
            rows_ref[slot, 1, t] = spread - high

    def on(n, ratio):
        source = lax.broadcasted_iota(jnp.int32, (n, rows), 1)
        return source // ratio == lax.broadcasted_iota(jnp.int32, (n, rows), 0)

    med_on, coarse_on = on(n_med, MED), on(n_coarse, COARSE)
    for h in range(heads):
        for copy in copies[h]:
            copy.wait()
        for t, ref in enumerate((k_ref, v_ref)):
            row = pl.ds(h, 1)
            left = []
            for part in range(2):
                left.append(jnp.where(med_on, rows_ref[0, part, t, row, :], 0.0))
                left.append(jnp.where(coarse_on, rows_ref[1, part, t, row, :], 0.0))
            r = mm(jnp.concatenate(left, axis=0).astype(BF16), ref[:, head_cols(h)])
            r = r[: n_med + n_coarse] + r[n_med + n_coarse :]
            med_ref[t, :, head_cols(h)] = r[:n_med].astype(BF16)
            coarse_ref[:, head_cols(t * heads + h)] = r[n_med:].astype(BF16)


def pool(keys, values, med_weight, coarse_weight):
    rows, width = keys.shape
    heads = width // HEAD_DIM
    return pl.pallas_call(
        functools.partial(pool_kernel, heads),
        out_shape=(jax.ShapeDtypeStruct((2, rows // MED, width), BF16),
            jax.ShapeDtypeStruct((rows // COARSE, 2 * width), BF16),
        ),
        in_specs=[HBM, HBM, VMEM, HBM],
        out_specs=(VMEM, VMEM),
        scratch_shapes=[
            pltpu.VMEM((rows, width), BF16),
            pltpu.VMEM((rows, width), BF16),
            pltpu.VMEM(coarse_weight.shape, F32),
            pltpu.VMEM((2, 2, 2, heads, rows), F32),
            pltpu.SemaphoreType.DMA((2, heads)),
            pltpu.SemaphoreType.DMA((1,)),
        ],
        compiler_params=pltpu.CompilerParams(vmem_limit_bytes=12 << 20),
        cost_estimate=pl.CostEstimate(
            flops=4 * 136 * rows * 2 * width, bytes_accessed=3 << 20, transcendentals=0
        ),
        name="pool",
    )(
        in_hbm(keys),
        in_hbm(values),
        med_weight,
        in_hbm(coarse_weight),
    )


def weigh(scores, peak, values):
    p = jnp.exp2((scores - peak) * EXP2_SCALE).astype(BF16)
    return mm(p, jnp.concatenate([values, jnp.ones_like(values)], axis=1))


def near_kernel(
    tile, heads,
    pos_ref, q_hbm, k_hbm, v_hbm, ek_hbm, ev_hbm,
    acc_hbm, peak_hbm,
    q_ref, k_ref, v_ref, acc_ref, peak_ref, sems, out_sems,
):
    rows, n_edge = q_ref.shape[0], ek_hbm.shape[0]
    own, edge = pl.ds(n_edge, rows), pl.ds(0, n_edge)
    copies = fetch_heads(
        (
            (q_hbm, q_ref),
            (k_hbm, k_ref.at[own, :]),
            (v_hbm, v_ref.at[own, :]),
            (ek_hbm, k_ref.at[edge, :]),
            (ev_hbm, v_ref.at[edge, :]),
        ),
        sems,
        heads,
    )
    has_edge = pos_ref[0] >= 1
    written = []
    on_diag = lax.broadcasted_iota(jnp.int32, (tile, tile), 1) <= lax.broadcasted_iota(
        jnp.int32, (tile, tile), 0
    )
    for h in range(heads):
        for copy in copies[h]:
            copy.wait()
        c = head_cols(h)
        for i in range(rows // tile):
            at, n = pl.ds(i * tile, tile), n_edge + i * tile
            s = mm_t(q_ref[at, c], k_ref[: n + tile, c])
            parts = [jnp.where(has_edge, s[:, :n_edge], NEG)]
            if i:
                parts.append(s[:, n_edge:n])
            parts.append(jnp.where(on_diag, s[:, n:], NEG))
            s = jnp.concatenate(parts, axis=1)
            peak = jnp.max(s, axis=1, keepdims=True)
            acc_ref[at, pl.ds(2 * h * HEAD_DIM, 2 * HEAD_DIM)] = weigh(
                s, peak, v_ref[: n + tile, c]
            )
            peak_ref[at, c] = jnp.broadcast_to(peak, (tile, HEAD_DIM))
        c2 = pl.ds(2 * h * HEAD_DIM, 2 * HEAD_DIM)
        written.append(
            [
                pltpu.make_async_copy(acc_ref.at[:, c2], acc_hbm.at[:, c2], out_sems.at[0, h]),
                pltpu.make_async_copy(peak_ref.at[:, c], peak_hbm.at[:, c], out_sems.at[1, h]),
            ]
        )
        for copy in written[h]:
            copy.start()
    for pair in written:
        for copy in pair:
            copy.wait()


def near(position, queries, keys, values, edge_keys, edge_values):
    rows, width = queries.shape
    heads = width // HEAD_DIM
    n_keys = edge_keys.shape[0] + rows
    return pl.pallas_call(
        functools.partial(near_kernel, 256, heads),
        out_shape=(pltpu.HBM((rows, 2 * width), F32), pltpu.HBM((rows, width), F32)),
        in_specs=[SMEM] + [HBM] * 5,
        out_specs=(HBM, HBM),
        scratch_shapes=[
            pltpu.VMEM((rows, width), BF16),
            pltpu.VMEM((n_keys, width), BF16),
            pltpu.VMEM((n_keys, width), BF16),
            pltpu.VMEM((rows, 2 * width), F32),
            pltpu.VMEM((rows, width), F32),
            pltpu.SemaphoreType.DMA((5, heads)),
            pltpu.SemaphoreType.DMA((2, heads)),
        ],
        compiler_params=pltpu.CompilerParams(vmem_limit_bytes=32 << 20),
        cost_estimate=pl.CostEstimate(
            flops=rows * n_keys * width, bytes_accessed=1 << 20, transcendentals=0
        ),
        name="near",
    )(position, *[in_hbm(x) for x in (queries, keys, values)], edge_keys, edge_values)


def far_kernel(
    first_row, heads, members, per_coarse,
    pos_ref, head_ref, q_hbm, m2, m3, m4, mine, other, acc_hbm, peak_hbm, w_hbm,
    att_ref, left_ref, right_ref,
    q_ref, k_ref, v_ref, acc_ref, peak_ref, w_ref, sems, w_sem,
):
    rows, width = att_ref.shape
    n_med, n_coarse = m2.shape[1], mine.shape[0]
    groups = heads // 2

    def whole(src, dst, g, per):
        cols = pl.ds(g * per, per)
        return src.at[pl.ds(first_row, rows), cols], dst.at[:, cols]

    def part(src, dst, g, to, shift=0):
        size = src.shape[0]
        return (
            src.at[:, pl.ds(shift + g * 2 * HEAD_DIM, 2 * HEAD_DIM)],
            dst.at[pl.ds(to, size), pl.ds(g * 2 * HEAD_DIM, 2 * HEAD_DIM)],
        )

    def group_copies(g):
        pairs = [whole(q_hbm, q_ref, g, 2 * HEAD_DIM)]
        to = 0
        for m in (m2, m3, m4):
            pairs += [part(m.at[0], k_ref, g, to), part(m.at[1], v_ref, g, to)]
            to += n_med
        for c in (mine, other):
            pairs += [part(c, k_ref, g, to), part(c, v_ref, g, to, width)]
            to += n_coarse
        pairs.append(whole(acc_hbm, acc_ref, g, 4 * HEAD_DIM))
        pairs.append(whole(peak_hbm, peak_ref, g, 2 * HEAD_DIM))
        return [
            pltpu.make_async_copy(src, dst, sems.at[t, g]) for t, (src, dst) in enumerate(pairs)
        ]

    copies = [group_copies(g) for g in range(groups)]

    def start(g):
        for copy in copies[g]:
            copy.start()

    block = lax.rem(head_ref[0] + 2, members)
    cols = pl.ds(pl.multiple_of(block * width, width), width)
    w_copy = pltpu.make_async_copy(w_hbm.at[:, cols], w_ref, w_sem.at[0])
    for g in range(2):
        start(g)
    w_copy.start()
    pos = pos_ref[0]
    j = lax.broadcasted_iota(jnp.int32, (1, n_coarse), 1) // per_coarse
    group = j // (2 * CHIPS_X)
    step = jnp.where(group == 3, -1, group)
    z = (pos // PLANE + step + 4 * (j % 2)) & (PLANES - 1)
    x = (pos % PLANE // 2 - j // 2 % CHIPS_X) & (CHIPS_X - 1)
    bias = [
        jnp.where(pos >= d, jnp.zeros((1, n_med), F32), jnp.full((1, n_med), NEG, F32))
        for d in (2, 3, 4)
    ]
    for core in (pos % 2, 1 - pos % 2):
        bias.append(jnp.where(z * PLANE + x * 2 + core < pos, 0.0, NEG))
    bias = jnp.concatenate(bias, axis=1)
    for h in range(heads):
        if h % 2 == 0:
            for copy in copies[h // 2]:
                copy.wait()
            if h // 2 + 2 < groups:
                start(h // 2 + 2)
        c = head_cols(h)
        s = mm_t(q_ref[:, c], k_ref[:, c]) + bias
        near_peak = peak_ref[:, c]
        peak = jnp.maximum(near_peak, jnp.max(s, axis=1, keepdims=True))
        shrink = jnp.exp2((near_peak - peak) * EXP2_SCALE)
        got = weigh(s, peak[:, :1], v_ref[:, c])
        near_acc = acc_ref[:, head_cols(2 * h)]
        near_total = acc_ref[:, head_cols(2 * h + 1)]
        att_ref[:, c] = (
            (near_acc * shrink + got[:, :HEAD_DIM]) / (near_total * shrink + got[:, HEAD_DIM:])
        ).astype(BF16)
    w_copy.wait()
    middle = width // 2
    left_ref[...] = mm(att_ref[...], w_ref[:, :middle]).astype(BF16)
    right_ref[...] = mm(att_ref[...], w_ref[:, middle:]).astype(BF16)


def far(position, head, queries, meds, coarse, acc, peak, weight, first_row, rows):
    block, width = queries.shape
    heads = width // HEAD_DIM
    members = weight.shape[1] // width
    n_keys = 3 * meds[0].shape[1] + 2 * coarse[0].shape[0]
    half = jax.ShapeDtypeStruct((rows, width // 2), BF16)
    return pl.pallas_call(
        functools.partial(far_kernel, first_row, heads, members, block // COARSE),
        out_shape=(jax.ShapeDtypeStruct((rows, width), BF16), half, half),
        in_specs=[SMEM, SMEM] + [HBM] * 9,
        out_specs=(VMEM, VMEM, VMEM),
        scratch_shapes=[
            pltpu.VMEM((rows, width), BF16),
            pltpu.VMEM((n_keys, width), BF16),
            pltpu.VMEM((n_keys, width), BF16),
            pltpu.VMEM((rows, 2 * width), F32),
            pltpu.VMEM((rows, width), F32),
            pltpu.VMEM((width, width), BF16),
            pltpu.SemaphoreType.DMA((13, heads // 2)),
            pltpu.SemaphoreType.DMA((1,)),
        ],
        compiler_params=pltpu.CompilerParams(vmem_limit_bytes=36 << 20),
        cost_estimate=pl.CostEstimate(
            flops=8 * rows * n_keys * width, bytes_accessed=2 << 20, transcendentals=0
        ),
        name="far",
    )(
        position,
        head,
        in_hbm(queries),
        in_hbm(meds[0]),
        meds[1],
        in_hbm(meds[2]),
        *coarse,
        in_hbm(acc),
        in_hbm(peak),
        in_hbm(weight),
    )


def project_kernel(members, order, head_ref, a_ref, w_hbm, *refs):
    outs, (w_ref, sems) = refs[: len(order)], refs[len(order) :]
    width = outs[0].shape[1]
    copies = []
    for i, k in enumerate(order):
        block = lax.rem(head_ref[0] + k, members)
        cols = pl.ds(pl.multiple_of(block * width, width), width)
        copies.append(pltpu.make_async_copy(w_hbm.at[:, cols], w_ref.at[i], sems.at[i]))
        copies[i].start()
    for i, out in enumerate(outs):
        copies[i].wait()
        out[...] = mm(a_ref[...], w_ref[i]).astype(BF16)


def project(head, attention, weight, members, order):
    rows, depth = attention.shape
    width = weight.shape[1] // members
    return pl.pallas_call(
        functools.partial(project_kernel, members, order),
        out_shape=[jax.ShapeDtypeStruct((rows, width), BF16)] * len(order),
        in_specs=[SMEM, VMEM, HBM],
        out_specs=[VMEM] * len(order),
        scratch_shapes=[
            pltpu.VMEM((len(order), depth, width), BF16),
            pltpu.SemaphoreType.DMA((len(order),)),
        ],
        compiler_params=pltpu.CompilerParams(vmem_limit_bytes=24 << 20),
        cost_estimate=pl.CostEstimate(
            flops=2 * rows * depth * width * len(order),
            bytes_accessed=6 << 20,
            transcendentals=0,
        ),
        name="project",
    )(head, attention, in_hbm(weight))


def shifted(block, axis, distance):
    devices = range(lax.axis_size(axis))
    return lax.ppermute(
        block, axis, [(i - distance, i) for i in devices if i - distance in devices]
    )


def body(queries, keys, values, med_weight, coarse_weight, out_weight):
    n_seq = lax.axis_size("seq")
    members = lax.axis_size("head")
    position = lax.axis_index("seq")
    pos = position.astype(jnp.int32).reshape(1)
    head = lax.axis_index("head").astype(jnp.int32).reshape(1)
    swap = [(i, i ^ 1) for i in range(n_seq)]

    def place(z, x, core):
        return z * PLANE + x * 2 + core

    def move(block, dz, dx):
        route = [
            (place(z, x, c), place((z + dz) % PLANES, (x + dx) % CHIPS_X, c))
            for z in range(PLANES)
            for x in range(CHIPS_X)
            for c in range(2)
        ]
        return lax.ppermute(block, "seq", route)

    edge_keys = shifted(keys, "seq", 1)
    med, coarse = pool(keys, values, med_weight, coarse_weight)
    quad = jnp.concatenate([coarse, move(coarse, 4, 0)], 0)
    ring = jnp.concatenate([quad] + [move(quad, 0, d) for d in range(1, CHIPS_X)], 0)

    edge_keys, values, ring, med = lax.optimization_barrier((edge_keys, values, ring, med))
    edge_values = shifted(values, "seq", 1)
    below = move(ring, -1, 0)
    turned = move(med, 0, -1)
    below, edge_values, turned, med, ring = lax.optimization_barrier(
        (below, edge_values, turned, med, ring)
    )
    med2 = shifted(med, "seq", 2)
    last = [
        (place(z, x, c), place(z + (x + 1) % CHIPS_X // 2, (x - 1) % CHIPS_X, c))
        for z in range(PLANES)
        for x in range(CHIPS_X)
        for c in range(2)
        if z + (x + 1) % CHIPS_X // 2 < PLANES
    ]
    med4 = lax.ppermute(turned, "seq", last)
    rings = [move(ring, d, 0) for d in (-2, 1)]
    acc, peak = near(pos, queries, keys, values, edge_keys, edge_values)
    rings, med2, med4, acc, peak = lax.optimization_barrier((rings, med2, med4, acc, peak))
    mine = jnp.concatenate([ring, below] + rings, 0)
    other = lax.ppermute(mine, "seq", swap)
    med3 = lax.ppermute(jnp.where(pos % 2 == 0, med2, med4), "seq", swap)

    def send(block, distance):
        return lax.ppermute(
            block, "head", [(i, (i + distance) % members) for i in range(members)]
        )

    def plus(*blocks):
        return functools.reduce(jnp.add, [x.astype(F32) for x in blocks]).astype(BF16)

    rows = queries.shape[0] // CHUNKS
    parts = []
    for c in range(CHUNKS):
        attention, left, right = far(
            pos,
            head,
            queries,
            (med2, med3, med4),
            (mine, other),
            acc,
            peak,
            out_weight,
            c * rows,
            rows,
        )
        attention, pos = lax.optimization_barrier((attention, pos))
        if parts:
            parts[-1], (attention, left, right) = lax.optimization_barrier(
                (parts[-1], (attention, left, right))
            )
        parts.append((attention, send(left, 1), send(right, -1)))
    pieces = []
    for attention, left, right in parts:
        if pieces:
            attention, left, right = lax.optimization_barrier((attention, left, right))
        ahead, behind, own = project(head, attention, out_weight, members, (1, members - 1, 0))
        middle = left.shape[1]
        ahead = jnp.concatenate([plus(ahead[:, :middle], left), ahead[:, middle:]], 1)
        behind = jnp.concatenate([behind[:, :middle], plus(behind[:, middle:], right)], 1)
        pieces.append(plus(own, send(ahead, 1), send(behind, -1)))
    return jnp.concatenate(pieces, axis=0)


def solution(mesh):
    placed = (
        P("seq", "head"),
        P("seq", "head"),
        P("seq", "head"),
        P(None, "head", None),
        P(None, "head", None),
        P("head", None),
    )
    return jax.shard_map(
        body, mesh=mesh, in_specs=placed, out_specs=P("seq", "head"), check_vma=False
    )
```

```python
import functools
import math

import jax
import jax.numpy as jnp
from jax import lax
from jax.experimental import pallas as pl
from jax.experimental.pallas import tpu as pltpu
from jax.sharding import PartitionSpec as P

HEAD_DIM = 128
WIN = 512
MED = 4
COARSE = 64
CHIPS_X = 4
PLANE = 2 * CHIPS_X
PLANES = 8
CHUNKS = 2
NEG = -1e30
EXP2_SCALE = math.log2(math.e) / math.sqrt(HEAD_DIM)
F32 = jnp.float32
BF16 = jnp.bfloat16
HBM = pl.BlockSpec(memory_space=pltpu.HBM)
VMEM = pl.BlockSpec(memory_space=pltpu.VMEM)
SMEM = pl.BlockSpec(memory_space=pltpu.SMEM)


def in_hbm(x):
    return pltpu.with_memory_space_constraint(x, pltpu.HBM)


def mm(a, b):
    return lax.dot_general(a, b, (((1,), (0,)), ((), ())), preferred_element_type=F32)


def mm_t(a, b):
    return lax.dot_general(a, b, (((1,), (1,)), ((), ())), preferred_element_type=F32)


def head_cols(h):
    return pl.ds(h * HEAD_DIM, HEAD_DIM)


def fetch_heads(pairs, sems, heads):
    copies = []
    for h in range(heads):
        copies.append(
            [
                pltpu.make_async_copy(
                    src.at[:, head_cols(h)], dst.at[:, head_cols(h)], sems.at[t, h]
                )
                for t, (src, dst) in enumerate(pairs)
            ]
        )
        for copy in copies[h]:
            copy.start()
    return copies


def pool_kernel(
    heads,
    k_hbm, v_hbm, mw_ref, cw_hbm,
    med_ref, coarse_ref,
    k_ref, v_ref, cw_ref, rows_ref, sems, w_sem,
):
    w_copy = pltpu.make_async_copy(cw_hbm, cw_ref, w_sem.at[0])
    w_copy.start()
    copies = fetch_heads(((k_hbm, k_ref), (v_hbm, v_ref)), sems, heads)
    rows = k_ref.shape[0]
    n_med, n_coarse = rows // MED, rows // COARSE
    lane = lax.broadcasted_iota(jnp.int32, (heads, rows), 1)
    for slot, (ref, ratio) in enumerate(((mw_ref, MED), (cw_ref, COARSE))):
        at = lane % ratio
        if slot:
            w_copy.wait()
        for t in range(2):
            w = ref[t]
            spread = jnp.zeros((heads, rows), F32)
            for r in range(ratio):
                spread = jnp.where(at == r, w[:, r : r + 1], spread)
            high = spread.astype(BF16).astype(F32)
            rows_ref[slot, 0, t] = high
            rows_ref[slot, 1, t] = spread - high

    def on(n, ratio):
        source = lax.broadcasted_iota(jnp.int32, (n, rows), 1)
        return source // ratio == lax.broadcasted_iota(jnp.int32, (n, rows), 0)

    med_on, coarse_on = on(n_med, MED), on(n_coarse, COARSE)
    for h in range(heads):
        for copy in copies[h]:
            copy.wait()
        for t, ref in enumerate((k_ref, v_ref)):
            row = pl.ds(h, 1)
            left = []
            for part in range(2):
                left.append(jnp.where(med_on, rows_ref[0, part, t, row, :], 0.0))
                left.append(jnp.where(coarse_on, rows_ref[1, part, t, row, :], 0.0))
            r = mm(jnp.concatenate(left, axis=0).astype(BF16), ref[:, head_cols(h)])
            r = r[: n_med + n_coarse] + r[n_med + n_coarse :]
            med_ref[t, :, head_cols(h)] = r[:n_med].astype(BF16)
            coarse_ref[:, head_cols(t * heads + h)] = r[n_med:].astype(BF16)


def pool(keys, values, med_weight, coarse_weight):
    rows, width = keys.shape
    heads = width // HEAD_DIM
    return pl.pallas_call(
        functools.partial(pool_kernel, heads),
        out_shape=(jax.ShapeDtypeStruct((2, rows // MED, width), BF16),
            jax.ShapeDtypeStruct((rows // COARSE, 2 * width), BF16),
        ),
        in_specs=[HBM, HBM, VMEM, HBM],
        out_specs=(VMEM, VMEM),
        scratch_shapes=[
            pltpu.VMEM((rows, width), BF16),
            pltpu.VMEM((rows, width), BF16),
            pltpu.VMEM(coarse_weight.shape, F32),
            pltpu.VMEM((2, 2, 2, heads, rows), F32),
            pltpu.SemaphoreType.DMA((2, heads)),
            pltpu.SemaphoreType.DMA((1,)),
        ],
        compiler_params=pltpu.CompilerParams(vmem_limit_bytes=12 << 20),
        cost_estimate=pl.CostEstimate(
            flops=4 * 136 * rows * 2 * width, bytes_accessed=3 << 20, transcendentals=0
        ),
        name="pool",
    )(
        in_hbm(keys),
        in_hbm(values),
        med_weight,
        in_hbm(coarse_weight),
    )


def weigh(scores, peak, values):
    p = jnp.exp2((scores - peak) * EXP2_SCALE).astype(BF16)
    return mm(p, jnp.concatenate([values, jnp.ones_like(values)], axis=1))


def near_kernel(
    tile, heads,
    pos_ref, q_hbm, k_hbm, v_hbm, ek_hbm, ev_hbm,
    acc_hbm, peak_hbm,
    q_ref, k_ref, v_ref, acc_ref, peak_ref, sems, out_sems,
):
    rows, n_edge = q_ref.shape[0], ek_hbm.shape[0]
    own, edge = pl.ds(n_edge, rows), pl.ds(0, n_edge)
    inputs = (
        (q_hbm, q_ref),
        (k_hbm, k_ref.at[own, :]),
        (v_hbm, v_ref.at[own, :]),
        (ek_hbm, k_ref.at[edge, :]),
        (ev_hbm, v_ref.at[edge, :]),
    )
    fetch_heads(inputs, sems, heads)
    has_edge = pos_ref[0] >= 1
    on_diag = lax.broadcasted_iota(jnp.int32, (tile, tile), 1) <= lax.broadcasted_iota(
        jnp.int32, (tile, tile), 0
    )

    def columns(h):
        return (
            pl.ds(pl.multiple_of(h * HEAD_DIM, HEAD_DIM), HEAD_DIM),
            pl.ds(pl.multiple_of(h * 2 * HEAD_DIM, 2 * HEAD_DIM), 2 * HEAD_DIM),
        )

    def written(h):
        c, c2 = columns(h)
        return (
            pltpu.make_async_copy(acc_ref.at[:, c2], acc_hbm.at[:, c2], out_sems.at[0, h]),
            pltpu.make_async_copy(peak_ref.at[:, c], peak_hbm.at[:, c], out_sems.at[1, h]),
        )

    def one_head(h):
        c, c2 = columns(h)
        for t, (src, dst) in enumerate(inputs):
            pltpu.make_async_copy(src.at[:, c], dst.at[:, c], sems.at[t, h]).wait()
        for i in range(rows // tile):
            at, n = pl.ds(i * tile, tile), n_edge + i * tile
            s = mm_t(q_ref[at, c], k_ref[: n + tile, c])
            parts = [jnp.where(has_edge, s[:, :n_edge], NEG)]
            if i:
                parts.append(s[:, n_edge:n])
            parts.append(jnp.where(on_diag, s[:, n:], NEG))
            s = jnp.concatenate(parts, axis=1)
            peak = jnp.max(s, axis=1, keepdims=True)
            acc_ref[at, c2] = weigh(s, peak, v_ref[: n + tile, c])
            peak_ref[at, c] = jnp.broadcast_to(peak, (tile, HEAD_DIM))
        for copy in written(h):
            copy.start()

    @pl.loop(0, heads // 2)
    def _(g):
        one_head(2 * g)
        one_head(2 * g + 1)

    for h in range(heads):
        for copy in written(h):
            copy.wait()


def near(position, queries, keys, values, edge_keys, edge_values):
    rows, width = queries.shape
    heads = width // HEAD_DIM
    n_keys = edge_keys.shape[0] + rows
    return pl.pallas_call(
        functools.partial(near_kernel, 256, heads),
        out_shape=(pltpu.HBM((rows, 2 * width), F32), pltpu.HBM((rows, width), F32)),
        in_specs=[SMEM] + [HBM] * 5,
        out_specs=(HBM, HBM),
        scratch_shapes=[
            pltpu.VMEM((rows, width), BF16),
            pltpu.VMEM((n_keys, width), BF16),
            pltpu.VMEM((n_keys, width), BF16),
            pltpu.VMEM((rows, 2 * width), F32),
            pltpu.VMEM((rows, width), F32),
            pltpu.SemaphoreType.DMA((5, heads)),
            pltpu.SemaphoreType.DMA((2, heads)),
        ],
        compiler_params=pltpu.CompilerParams(vmem_limit_bytes=32 << 20),
        cost_estimate=pl.CostEstimate(
            flops=rows * n_keys * width, bytes_accessed=1 << 20, transcendentals=0
        ),
        name="near",
    )(position, *[in_hbm(x) for x in (queries, keys, values)], edge_keys, edge_values)


def far_kernel(
    first_row, heads, members, per_coarse,
    pos_ref, head_ref, q_hbm, m2, m3, m4, mine, other, acc_hbm, peak_hbm, w_hbm,
    att_ref, left_ref, right_ref,
    q_ref, k_ref, v_ref, acc_ref, peak_ref, w_ref, sems, w_sem,
):
    rows, width = att_ref.shape
    n_med, n_coarse = m2.shape[1], mine.shape[0]
    groups = heads // 2

    def whole(src, dst, g, per):
        cols = pl.ds(g * per, per)
        return src.at[pl.ds(first_row, rows), cols], dst.at[:, cols]

    def part(src, dst, g, to, shift=0):
        size = src.shape[0]
        return (
            src.at[:, pl.ds(shift + g * 2 * HEAD_DIM, 2 * HEAD_DIM)],
            dst.at[pl.ds(to, size), pl.ds(g * 2 * HEAD_DIM, 2 * HEAD_DIM)],
        )

    def group_copies(g):
        pairs = [whole(q_hbm, q_ref, g, 2 * HEAD_DIM)]
        to = 0
        for m in (m2, m3, m4):
            pairs += [part(m.at[0], k_ref, g, to), part(m.at[1], v_ref, g, to)]
            to += n_med
        for c in (mine, other):
            pairs += [part(c, k_ref, g, to), part(c, v_ref, g, to, width)]
            to += n_coarse
        pairs.append(whole(acc_hbm, acc_ref, g, 4 * HEAD_DIM))
        pairs.append(whole(peak_hbm, peak_ref, g, 2 * HEAD_DIM))
        return [
            pltpu.make_async_copy(src, dst, sems.at[t, g]) for t, (src, dst) in enumerate(pairs)
        ]

    copies = [group_copies(g) for g in range(groups)]

    def start(g):
        for copy in copies[g]:
            copy.start()

    block = lax.rem(head_ref[0] + 2, members)
    cols = pl.ds(pl.multiple_of(block * width, width), width)
    w_copy = pltpu.make_async_copy(w_hbm.at[:, cols], w_ref, w_sem.at[0])
    for g in range(2):
        start(g)
    w_copy.start()
    pos = pos_ref[0]
    j = lax.broadcasted_iota(jnp.int32, (1, n_coarse), 1) // per_coarse
    group = j // (2 * CHIPS_X)
    step = jnp.where(group == 3, -1, group)
    z = (pos // PLANE + step + 4 * (j % 2)) & (PLANES - 1)
    x = (pos % PLANE // 2 - j // 2 % CHIPS_X) & (CHIPS_X - 1)
    bias = [
        jnp.where(pos >= d, jnp.zeros((1, n_med), F32), jnp.full((1, n_med), NEG, F32))
        for d in (2, 3, 4)
    ]
    for core in (pos % 2, 1 - pos % 2):
        bias.append(jnp.where(z * PLANE + x * 2 + core < pos, 0.0, NEG))
    bias = jnp.concatenate(bias, axis=1)
    for h in range(heads):
        if h % 2 == 0:
            for copy in copies[h // 2]:
                copy.wait()
            if h // 2 + 2 < groups:
                start(h // 2 + 2)
        c = head_cols(h)
        s = mm_t(q_ref[:, c], k_ref[:, c]) + bias
        near_peak = peak_ref[:, c]
        peak = jnp.maximum(near_peak, jnp.max(s, axis=1, keepdims=True))
        shrink = jnp.exp2((near_peak - peak) * EXP2_SCALE)
        got = weigh(s, peak[:, :1], v_ref[:, c])
        near_acc = acc_ref[:, head_cols(2 * h)]
        near_total = acc_ref[:, head_cols(2 * h + 1)]
        att_ref[:, c] = (
            (near_acc * shrink + got[:, :HEAD_DIM]) / (near_total * shrink + got[:, HEAD_DIM:])
        ).astype(BF16)
    w_copy.wait()
    middle = width // 2
    left_ref[...] = mm(att_ref[...], w_ref[:, :middle]).astype(BF16)
    right_ref[...] = mm(att_ref[...], w_ref[:, middle:]).astype(BF16)


def far(position, head, queries, meds, coarse, acc, peak, weight, first_row, rows):
    block, width = queries.shape
    heads = width // HEAD_DIM
    members = weight.shape[1] // width
    n_keys = 3 * meds[0].shape[1] + 2 * coarse[0].shape[0]
    half = jax.ShapeDtypeStruct((rows, width // 2), BF16)
    return pl.pallas_call(
        functools.partial(far_kernel, first_row, heads, members, block // COARSE),
        out_shape=(jax.ShapeDtypeStruct((rows, width), BF16), half, half),
        in_specs=[SMEM, SMEM] + [HBM] * 9,
        out_specs=(VMEM, VMEM, VMEM),
        scratch_shapes=[
            pltpu.VMEM((rows, width), BF16),
            pltpu.VMEM((n_keys, width), BF16),
            pltpu.VMEM((n_keys, width), BF16),
            pltpu.VMEM((rows, 2 * width), F32),
            pltpu.VMEM((rows, width), F32),
            pltpu.VMEM((width, width), BF16),
            pltpu.SemaphoreType.DMA((13, heads // 2)),
            pltpu.SemaphoreType.DMA((1,)),
        ],
        compiler_params=pltpu.CompilerParams(vmem_limit_bytes=36 << 20),
        cost_estimate=pl.CostEstimate(
            flops=8 * rows * n_keys * width, bytes_accessed=2 << 20, transcendentals=0
        ),
        name="far",
    )(
        position,
        head,
        in_hbm(queries),
        in_hbm(meds[0]),
        meds[1],
        in_hbm(meds[2]),
        *coarse,
        in_hbm(acc),
        in_hbm(peak),
        in_hbm(weight),
    )


def project_kernel(members, order, head_ref, a_ref, w_hbm, *refs):
    outs, (w_ref, sems) = refs[: len(order)], refs[len(order) :]
    width = outs[0].shape[1]
    copies = []
    for i, k in enumerate(order):
        block = lax.rem(head_ref[0] + k, members)
        cols = pl.ds(pl.multiple_of(block * width, width), width)
        copies.append(pltpu.make_async_copy(w_hbm.at[:, cols], w_ref.at[i], sems.at[i]))
        copies[i].start()
    for i, out in enumerate(outs):
        copies[i].wait()
        out[...] = mm(a_ref[...], w_ref[i]).astype(BF16)


def project(head, attention, weight, members, order):
    rows, depth = attention.shape
    width = weight.shape[1] // members
    return pl.pallas_call(
        functools.partial(project_kernel, members, order),
        out_shape=[jax.ShapeDtypeStruct((rows, width), BF16)] * len(order),
        in_specs=[SMEM, VMEM, HBM],
        out_specs=[VMEM] * len(order),
        scratch_shapes=[
            pltpu.VMEM((len(order), depth, width), BF16),
            pltpu.SemaphoreType.DMA((len(order),)),
        ],
        compiler_params=pltpu.CompilerParams(vmem_limit_bytes=24 << 20),
        cost_estimate=pl.CostEstimate(
            flops=2 * rows * depth * width * len(order),
            bytes_accessed=6 << 20,
            transcendentals=0,
        ),
        name="project",
    )(head, attention, in_hbm(weight))


def shifted(block, axis, distance):
    devices = range(lax.axis_size(axis))
    return lax.ppermute(
        block, axis, [(i - distance, i) for i in devices if i - distance in devices]
    )


def body(queries, keys, values, med_weight, coarse_weight, out_weight):
    n_seq = lax.axis_size("seq")
    members = lax.axis_size("head")
    position = lax.axis_index("seq")
    pos = position.astype(jnp.int32).reshape(1)
    head = lax.axis_index("head").astype(jnp.int32).reshape(1)
    swap = [(i, i ^ 1) for i in range(n_seq)]

    def place(z, x, core):
        return z * PLANE + x * 2 + core

    def move(block, dz, dx):
        route = [
            (place(z, x, c), place((z + dz) % PLANES, (x + dx) % CHIPS_X, c))
            for z in range(PLANES)
            for x in range(CHIPS_X)
            for c in range(2)
        ]
        return lax.ppermute(block, "seq", route)

    edge_keys = shifted(keys, "seq", 1)
    med, coarse = pool(keys, values, med_weight, coarse_weight)
    quad = jnp.concatenate([coarse, move(coarse, 4, 0)], 0)
    ring = jnp.concatenate([quad] + [move(quad, 0, d) for d in range(1, CHIPS_X)], 0)

    edge_keys, values, ring, med = lax.optimization_barrier((edge_keys, values, ring, med))
    edge_values = shifted(values, "seq", 1)
    below = move(ring, -1, 0)
    turned = move(med, 0, -1)
    below, edge_values, turned, med, ring = lax.optimization_barrier(
        (below, edge_values, turned, med, ring)
    )
    med2 = shifted(med, "seq", 2)
    last = [
        (place(z, x, c), place(z + (x + 1) % CHIPS_X // 2, (x - 1) % CHIPS_X, c))
        for z in range(PLANES)
        for x in range(CHIPS_X)
        for c in range(2)
        if z + (x + 1) % CHIPS_X // 2 < PLANES
    ]
    med4 = lax.ppermute(turned, "seq", last)
    rings = [move(ring, d, 0) for d in (-2, 1)]
    acc, peak = near(pos, queries, keys, values, edge_keys, edge_values)
    rings, med2, med4, acc, peak = lax.optimization_barrier((rings, med2, med4, acc, peak))
    mine = jnp.concatenate([ring, below] + rings, 0)
    other = lax.ppermute(mine, "seq", swap)
    med3 = lax.ppermute(jnp.where(pos % 2 == 0, med2, med4), "seq", swap)

    def send(block, distance):
        return lax.ppermute(
            block, "head", [(i, (i + distance) % members) for i in range(members)]
        )

    def plus(*blocks):
        return functools.reduce(jnp.add, [x.astype(F32) for x in blocks]).astype(BF16)

    rows = queries.shape[0] // CHUNKS
    parts = []
    for c in range(CHUNKS):
        attention, left, right = far(
            pos,
            head,
            queries,
            (med2, med3, med4),
            (mine, other),
            acc,
            peak,
            out_weight,
            c * rows,
            rows,
        )
        attention, pos = lax.optimization_barrier((attention, pos))
        if parts:
            parts[-1], (attention, left, right) = lax.optimization_barrier(
                (parts[-1], (attention, left, right))
            )
        parts.append((attention, send(left, 1), send(right, -1)))
    pieces = []
    for attention, left, right in parts:
        if pieces:
            attention, left, right = lax.optimization_barrier((attention, left, right))
        ahead, behind, own = project(head, attention, out_weight, members, (1, members - 1, 0))
        middle = left.shape[1]
        ahead = jnp.concatenate([plus(ahead[:, :middle], left), ahead[:, middle:]], 1)
        behind = jnp.concatenate([behind[:, :middle], plus(behind[:, middle:], right)], 1)
        pieces.append(plus(own, send(ahead, 1), send(behind, -1)))
    return jnp.concatenate(pieces, axis=0)


def solution(mesh):
    placed = (
        P("seq", "head"),
        P("seq", "head"),
        P("seq", "head"),
        P(None, "head", None),
        P(None, "head", None),
        P("head", None),
    )
    return jax.shard_map(
        body, mesh=mesh, in_specs=placed, out_specs=P("seq", "head"), check_vma=False
    )
```
